256 devices in a mesh: wide: 64 (over z, y, core), narrow: 4 (over x).
Axes of the slice: x: 4, y: 4, z: 8, core: 2. Of those that a mesh axis runs over, the one named last changes fastest.
Arguments:
- hidden_in: bfloat16 [1024, 4096], P('narrow', 'wide'), may hold values from -0.59765625 to 0.59765625
- cached_len: int32 [4], replicated, may hold values from 1 to 4096, 8192 in all
- k_cache: bfloat16 [4, 32768, 128], P('narrow', 'wide'), may hold values from -256 to 256
- v_cache: bfloat16 [4, 32768, 128], P('narrow', 'wide'), may hold values from -24 to 24
- attn_gain: bfloat16 [4096], replicated, may hold values from 0.099609375 to 1.8984375
- ffn_gain: bfloat16 [4096], replicated, may hold values from 0.099609375 to 1.8984375
- wqkv: bfloat16 [6144, 4096], P('wide', 'narrow'), may hold values from -0.09375 to 0.09375
- wo: bfloat16 [4096, 4096], P('wide', 'narrow'), may hold values from -0.09375 to 0.09375
- wgate: bfloat16 [14336, 4096], P('wide', 'narrow'), may hold values from -0.09375 to 0.09375
- wup: bfloat16 [14336, 4096], P('wide', 'narrow'), may hold values from -0.09375 to 0.09375
- wdown: bfloat16 [14336, 4096], P('wide', 'narrow'), may hold values from -0.125 to 0.125
Outputs:
- hidden_out: bfloat16 [1024, 4096], P('narrow', 'wide')
- new_k_cache: bfloat16 [4, 32768, 128], P('narrow', 'wide')
- new_v_cache: bfloat16 [4, 32768, 128], P('narrow', 'wide')
The draws below stay inside these ranges and needn't reach their ends.
All inputs are finite; a program needn't handle non-finite values.
Results may differ from the reference program's by a relative error of at most 0.018.
The reference program's roundings to bfloat16 on the way (of `normed_attn`, `qkv`, `weights`, `attended`, `after_attn`, `normed_ffn` and `activation`) count: a program that leaves them out, or rounds other values in their place, can miss the bound.
Values may be sent and summed in bfloat16 or wider, within the bound.
A program may use at most 64 MiB of HBM per device.

```python
import math
import jax
import jax.numpy as jnp
import numpy as np
from jax import lax

D = 4096
QH = 32
KVH = 8
HD = 128
FF = 14336
WINDOW = 4096
SPAN = 256
REQ = 4
QKVW = 6144
TOKENS = 1024


def draw_k_cache(key, part):
    base_key = jax.random.fold_in(key, 11)
    values = jnp.clip(jax.random.normal(base_key, (REQ, KVH * WINDOW, HD), jnp.float32), -4.0, 4.0)
    return values.astype(jnp.bfloat16)


def spiked(array, own_key, source, target, parts, factor):
    owner, partner = [(jnp.arange(array.shape[dim]) // (array.shape[dim] // parts)).reshape([-1 if axis == dim else 1 for axis in range(array.ndim)]) for dim in (source, target)]
    chosen = jax.random.permutation(own_key, parts)[partner]
    strong = (owner == chosen) | (owner == (partner + parts // 2) % parts)
    return jnp.where(strong, factor * array, array)


def steps_of(stream_key, dims, pieces, smallest, largest):
    def one(position, blocks):
        steps = jax.random.uniform(jax.random.fold_in(jax.random.fold_in(stream_key, 6), position), (blocks,), jnp.float32, smallest / len(pieces), largest / len(pieces))
        return jnp.repeat(jnp.exp(steps), dims[position] // blocks).reshape((-1,) + (1,) * (len(dims) - position - 1))

    factor_of = one(*pieces[0])
    for cut in pieces[1:]:
        factor_of = factor_of * one(*cut)
    return factor_of


def profile(number_of, total, limit, lean):
    weights = [(1 << 20) // math.isqrt(standing ** lean) + 1 for standing in range(2, number_of + 1)]
    rest, holding = total - limit - (number_of - 1), [1] * (number_of - 1)
    while rest > 0:
        movable = [i for i in range(number_of - 1) if holding[i] < limit]
        mass, remaining = sum([weights[i] for i in movable]), rest
        for i in movable:
            addition = min(limit - holding[i], max(1, remaining * weights[i] // mass), rest)
            holding[i] = holding[i] + addition
            rest = rest - addition
    return np.array([limit] + holding)


def uneven_parts(rng, count, total, most, slope):
    if count == 2:
        one = jax.random.randint(rng, (), max(1, total - most), min(most, total - 1) + 1)
        return jnp.stack([one, total - one])
    sizes = jnp.asarray(profile(count, total, most, slope), jnp.int32)
    twos = (count - 1) // 2
    source_of, sink = sizes[1:1 + 2 * twos:2], sizes[2:2 + 2 * twos:2]
    slack = jnp.minimum(source_of - 1, most - sink)
    passed = jax.random.randint(jax.random.fold_in(rng, 1), (twos,), 0, 1 << 20) % (slack + 1)
    sizes = sizes.at[1:1 + 2 * twos:2].set(source_of - passed).at[2:2 + 2 * twos:2].set(sink + passed)
    return sizes[jax.random.permutation(jax.random.fold_in(rng, 2), count)]


def centred(stream_key, extent, spread, most, split=(), held_as=jnp.bfloat16):
    result = jax.random.normal(stream_key, extent, jnp.float32) * spread
    if len(split) > 0:
        result = steps_of(stream_key, extent, split, -0.22, 0.18) * result
    return jnp.clip(result, min=-most, max=most).astype(held_as)


def gaussian_with(stream_key, dims, scale, bound, split, heavy, kind=jnp.bfloat16):
    entries = scale * jax.random.normal(stream_key, dims, jnp.float32)
    if split:
        entries = entries * steps_of(stream_key, dims, split, -0.22, 0.18)
    return jnp.clip(spiked(entries, jax.random.fold_in(stream_key, 3), *heavy), -bound, bound).astype(kind)


def setup_inputs(seed: int = 0) -> dict:
    key_of = jax.random.split(jax.random.key(seed), 12)
    return {
        "hidden_in": centred(key_of[0], (TOKENS, D), 0.1, 0.59765625, ((0, 4), (1, 64))),
        "cached_len": uneven_parts(key_of[1], REQ, 2 * WINDOW, WINDOW, 2).astype(jnp.int32),
        "k_cache": draw_k_cache(jax.random.fold_in(key_of[11], 71), 0),
        "v_cache": centred(key_of[3], (REQ, KVH * WINDOW, HD), 4.0, 24.0, ((0, 4), (1, 64))),
        "attn_gain": jnp.clip(1.0 + 0.18 * jax.random.normal(key_of[4], (D,), jnp.float32), 0.099609375, 1.8984375).astype(jnp.bfloat16),
        "ffn_gain": jnp.clip(1.0 + 0.18 * jax.random.normal(key_of[5], (D,), jnp.float32), 0.099609375, 1.8984375).astype(jnp.bfloat16),
        "wqkv": centred(key_of[6], (QKVW, D), D ** -0.5, 0.09375, ((0, 64), (1, 4))),
        "wo": centred(key_of[7], (D, QH * HD), (QH * HD) ** -0.5, 0.09375, ((0, 64), (1, 4))),
        "wgate": centred(key_of[8], (FF, D), D ** -0.5, 0.09375, ((0, 64), (1, 4))),
        "wup": centred(key_of[9], (FF, D), D ** -0.5, 0.09375, ((0, 64), (1, 4))),
        "wdown": gaussian_with(key_of[10], (FF, D), FF ** -0.5, 0.125, ((0, 64), (1, 4)), (0, 1, 64, 4.0)),
    }


NEG_FILL = -1e+30

def rms_scale(values, weights):
    widened = values.astype(jnp.float32)
    mean_square = lax.optimization_barrier(jnp.mean(widened * widened, axis=-1, keepdims=True))
    return (widened * lax.rsqrt(mean_square + 1e-05) * weights.astype(jnp.float32)).astype(jnp.bfloat16)

def times_rows(left, right):
    return lax.dot_general(left, right, (((1,), (1,)), ((), ())), preferred_element_type=jnp.float32)

def rotate(heads, positions):
    half_width = heads.shape[-1] // 2
    exponent = jnp.arange(half_width, dtype=jnp.float32) * (2.0 / heads.shape[-1])
    frequency = jnp.power(10000.0, -exponent)
    angles = positions.astype(jnp.float32)[:, None] * frequency[None, :]
    cosine = jnp.cos(angles)[:, None, :]
    sine = jnp.sin(angles)[:, None, :]
    widened = heads.astype(jnp.float32)
    first_half = widened[..., :half_width]
    second_half = widened[..., half_width:]
    return jnp.concatenate([first_half * cosine - second_half * sine, second_half * cosine + first_half * sine], axis=-1).astype(jnp.bfloat16)

def reference(hidden_in, cached_len, k_cache, v_cache, attn_gain, ffn_gain, wqkv, wo, wgate, wup, wdown):
    group_size = QH // KVH
    normed_attn = rms_scale(hidden_in, attn_gain)
    qkv = times_rows(normed_attn, wqkv).astype(jnp.bfloat16)
    qkv = qkv.reshape(REQ, SPAN, KVH, group_size + 2, HD)
    keys_old = k_cache.reshape(REQ, KVH, WINDOW, HD)
    vals_old = v_cache.reshape(REQ, KVH, WINDOW, HD)
    slots = jnp.arange(WINDOW, dtype=jnp.int32)
    steps_t = jnp.arange(SPAN, dtype=jnp.int32)
    attended_list = []
    key_list = []
    value_list = []
    for request in range(REQ):
        length = cached_len[request]
        positions = length + steps_t
        block = qkv[request]
        queries = rotate(block[:, :, :group_size].reshape(SPAN, QH, HD), positions).reshape(SPAN, KVH, group_size, HD)
        new_keys = rotate(block[:, :, group_size], positions)
        new_vals = block[:, :, group_size + 1]
        cache_live = (slots[None, :] < length) & (slots[None, :] > positions[:, None] - WINDOW)
        new_live = steps_t[None, :] <= steps_t[:, None]
        allowed = jnp.concatenate([cache_live, new_live], axis=1)[:, None, :]
        head_outputs = []
        for head in range(KVH):
            all_keys = jnp.concatenate([keys_old[request, head], new_keys[:, head]], axis=0).astype(jnp.float32)
            all_vals = jnp.concatenate([vals_old[request, head], new_vals[:, head]], axis=0).astype(jnp.float32)
            scores = jnp.einsum('tgd,sd->tgs', queries[:, head].astype(jnp.float32), all_keys) * HD ** (-0.5)
            scores = jnp.where(allowed, scores, NEG_FILL)
            highest = lax.optimization_barrier(jnp.max(scores, axis=-1, keepdims=True))
            exp_terms = jnp.where(allowed, jnp.exp(scores - highest), 0.0)
            totals = lax.optimization_barrier(jnp.sum(exp_terms, axis=-1))
            weights = lax.optimization_barrier(exp_terms.astype(jnp.bfloat16)).astype(jnp.float32)
            mixed = jnp.einsum('tgs,sd->tgd', weights, all_vals)
            head_outputs.append(mixed / totals[..., None])
        attended_list.append(jnp.stack(head_outputs, axis=1).reshape(SPAN, QH * HD).astype(jnp.bfloat16))
        offset = (slots - length) % WINDOW
        fresh_slot = offset < SPAN
        pick_row = jnp.minimum(offset, SPAN - 1)
        key_list.append(jnp.where(fresh_slot[None, :, None], jnp.transpose(new_keys, (1, 0, 2))[:, pick_row], keys_old[request]))
        value_list.append(jnp.where(fresh_slot[None, :, None], jnp.transpose(new_vals, (1, 0, 2))[:, pick_row], vals_old[request]))
    attended = jnp.concatenate(attended_list, axis=0)
    after_attn = (hidden_in.astype(jnp.float32) + times_rows(attended, wo)).astype(jnp.bfloat16)
    normed_ffn = rms_scale(after_attn, ffn_gain)
    gate_proj = times_rows(normed_ffn, wgate)
    up_proj = times_rows(normed_ffn, wup)
    activation = (jax.nn.silu(gate_proj) * up_proj).astype(jnp.bfloat16)
    down_proj = jnp.dot(activation, wdown, preferred_element_type=jnp.float32)
    hidden_out = (after_attn.astype(jnp.float32) + down_proj).astype(jnp.bfloat16)
    new_k_cache = jnp.stack(key_list, axis=0).reshape(REQ, KVH * WINDOW, HD)
    new_v_cache = jnp.stack(value_list, axis=0).reshape(REQ, KVH * WINDOW, HD)
    return (hidden_out, new_k_cache, new_v_cache)
```

```python
import jax
import jax.numpy as jnp
from jax import lax
from jax.experimental import pallas as pl
from jax.experimental.pallas import tpu as pltpu
from jax.sharding import PartitionSpec as P

HD = 128
WINDOW = 4096
NEG_FILL = -1e30
NZ, NY, NX = 8, 4, 4
CHIPS = NZ * NY
TOK = 128
SLOTS = 512
BF16 = jnp.bfloat16
F32 = jnp.float32
YORDER = (0, 1, 3, 2)


def dot(a, b):
    return jnp.dot(a, b, preferred_element_type=F32)


def dot_nt(a, b):
    return lax.dot_general(a, b, (((1,), (1,)), ((), ())), preferred_element_type=F32)


def layer_kernel(
    len_ref, ht, cos, sin, gain1, gain2, kc, vc, wqkv, wo, wg, wu, wd,
    out, nk, nv,
    xb, ab, hb, nb, gq, kvn, krt, ka, vt, sc, sn, ssq,
    wqf, wof, wgf, wuf, wdf, gu, db, ra, rb, sa, sb, ys, yr, fin, fin_r,
    p_s, p_r, ag_s, ag_r, w_l, w_s, w_r, kv_s, kv_r, q_s, q_r, rs_s, rs_r,
):
    wide = lax.axis_index("wide")
    x = lax.axis_index("narrow")
    k = wide % 2
    y = (wide // 2) % NY
    z = wide // (2 * NY)
    sg = 1 - 2 * k
    chip = z * NY + y

    def dev(zz, yy, kk, xx):
        return {"wide": (zz * NY + yy) * 2 + kk, "narrow": xx}

    def ypeer(d):
        return dev(z, (y + d) % NY, k, x)

    partner = dev(z, y, 1 - k, x)
    za = (z + sg + NZ) % NZ
    zb = (z - sg + NZ) % NZ
    dev_a = dev(za, y, k, x)
    dev_b = dev(zb, y, k, x)
    xr = (x + 1) % NX
    xl = (x + NX - 1) % NX
    xo = (x + 2) % NX
    dev_xr = dev(z, y, k, xr)
    dev_xl = dev(z, y, k, xl)

    pending = []

    def send(src, dst, s_sem, r_sem, device):
        copy = pltpu.make_async_remote_copy(
            src_ref=src, dst_ref=dst, send_sem=s_sem, recv_sem=r_sem,
            device_id=device, device_id_type=pl.DeviceIdType.MESH,
        )
        copy.start()
        pending.append(copy)

    def arrive(dst, r_sem):
        pltpu.make_async_remote_copy(
            src_ref=dst, dst_ref=dst, send_sem=r_sem, recv_sem=r_sem,
            device_id=partner, device_id_type=pl.DeviceIdType.MESH,
        ).wait_recv()

    barrier = pltpu.get_barrier_semaphore()
    greet = [partner, ypeer(1), ypeer(2), ypeer(3), dev_a, dev_b, dev_xr, dev_xl]
    for peer in greet:
        pl.semaphore_signal(barrier, inc=1, device_id=peer, device_id_type=pl.DeviceIdType.MESH)
    vt[2 * y + k] = jnp.transpose(vc[...].astype(F32)).astype(BF16)
    ka[2 * y + k] = kc[...]
    ssq[...] = jnp.zeros_like(ssq)
    pl.semaphore_wait(barrier, len(greet))

    own_w = (wqkv, wo, wg, wu, wd)
    full_w = (wqf, wof, wgf, wuf, wdf)
    locals_w = []

    def w_first(m):
        f, o = full_w[m], own_w[m]
        copy = pltpu.make_async_copy(o, f.at[x, k], w_l.at[m])
        copy.start()
        locals_w.append(copy)
        send(o, f.at[x, k], w_s.at[m, 0], w_r.at[m, 0], dev_xr)
        send(o, f.at[x, k], w_s.at[m, 1], w_r.at[m, 1], dev_xl)
        send(o, f.at[x, k], w_s.at[m, 4], w_r.at[m, 4], partner)

    def w_second(m):
        f = full_w[m]
        half = f.shape[2] // 2
        lo, hi = pl.ds(0, half), pl.ds(half, half)
        arrive(f.at[xl, k], w_r.at[m, 0])
        send(f.at[xl, k, lo], f.at[xl, k, lo], w_s.at[m, 2], w_r.at[m, 2], dev_xr)
        send(f.at[xl, k], f.at[xl, k], w_s.at[m, 5], w_r.at[m, 5], partner)
        arrive(f.at[xr, k], w_r.at[m, 1])
        send(f.at[xr, k, hi], f.at[xr, k, hi], w_s.at[m, 3], w_r.at[m, 3], dev_xl)
        send(f.at[xr, k], f.at[xr, k], w_s.at[m, 6], w_r.at[m, 6], partner)

    def w_third(m):
        f = full_w[m]
        half = f.shape[2] // 2
        lo, hi = pl.ds(0, half), pl.ds(half, half)
        arrive(f.at[xo, k, lo], w_r.at[m, 2])
        arrive(f.at[xo, k, hi], w_r.at[m, 3])
        send(f.at[xo, k], f.at[xo, k], w_s.at[m, 7], w_r.at[m, 7], partner)

    def w_ready(m):
        f = full_w[m]
        locals_w[m].wait()
        for i, block in enumerate((x, xl, xr, xo)):
            arrive(f.at[block, 1 - k], w_r.at[m, 4 + i])

    def all_gather(g, buf, on_chunk, extra, pumps):
        send_sem, recv_sem = ag_s.at[g], ag_r.at[g]

        def a_sem(s, d):
            return 3 + (s - 1) * 4 + d

        def b_sem(s, d):
            return 19 + (s - 1) * 4 + d

        def row(zz, d):
            return ((zz + 2 * NZ) % NZ) * NY + (y + NY - d) % NY

        def push_a(s, d):
            ref = buf.at[row(z - sg * (s - 1), d)]
            send(ref, ref, send_sem.at[a_sem(s, d)], recv_sem.at[a_sem(s, d)], dev_a)

        def push_b(s, d):
            ref = buf.at[row(z + sg * (s - 1), d)]
            send(ref, ref, send_sem.at[b_sem(s, d)], recv_sem.at[b_sem(s, d)], dev_b)

        own = buf.at[chip]
        for d in (1, 3, 2):
            send(own, own, send_sem.at[d - 1], recv_sem.at[d - 1], ypeer(d))
        push_a(1, 0)
        push_b(1, 0)
        extra()
        on_chunk(chip)
        for d in YORDER[1:]:
            arrive(buf.at[row(z, d)], recv_sem.at[d - 1])
            push_a(1, d)
            push_b(1, d)
            on_chunk(row(z, d))
        for s in range(2, 6):
            for d in YORDER:
                c = row(z - sg * (s - 1), d)
                arrive(buf.at[c], recv_sem.at[a_sem(s - 1, d)])
                if s <= 4:
                    push_a(s, d)
                on_chunk(c)
                if s <= 4:
                    c = row(z + sg * (s - 1), d)
                    arrive(buf.at[c], recv_sem.at[b_sem(s - 1, d)])
                    if s <= 3:
                        push_b(s, d)
                    on_chunk(c)
            if s in pumps:
                pumps[s]()

    def add_square(buf):
        def run(c):
            v = buf[c].astype(F32)
            ssq[...] += jnp.sum((v * v).reshape(16, 8, TOK), axis=0)

        return run

    def normalise(buf, gain):
        mean_square = jnp.sum(ssq[...], axis=0, keepdims=True) * (1.0 / (CHIPS * 128))
        r = lax.rsqrt(mean_square + 1e-05)
        gains = gain[...]
        for c in range(CHIPS):
            nb[c] = (buf[c].astype(F32) * r * gains[:, c : c + 1]).astype(BF16)

    half_rows = pl.ds(pl.multiple_of(k * 64, 64), 64)
    other_rows = pl.ds(pl.multiple_of((1 - k) * 64, 64), 64)
    send(ht.at[1 - k], xb.at[chip, half_rows], p_s.at[0], p_r.at[0], partner)
    xb[chip, half_rows, :] = ht[k]
    w_first(0)
    w_first(1)
    arrive(xb.at[chip, other_rows], p_r.at[0])

    def send_caches():
        p = 2 * y + k
        for d in (1, 3, 2):
            send(ka.at[p], ka.at[p], kv_s.at[0, d - 1], kv_r.at[0, d - 1], ypeer(d))
            send(vt.at[p], vt.at[p], kv_s.at[1, d - 1], kv_r.at[1, d - 1], ypeer(d))
        send(ka.at[p], ka.at[p], kv_s.at[0, 3], kv_r.at[0, 3], partner)
        send(vt.at[p], vt.at[p], kv_s.at[1, 3], kv_r.at[1, 3], partner)

    def pass_caches():
        for d in (1, 3, 2):
            p = 2 * ((y + NY - d) % NY) + k
            for i, buf in enumerate((ka, vt)):
                arrive(buf.at[p], kv_r.at[i, d - 1])
                send(buf.at[p], buf.at[p], kv_s.at[i, 3 + d], kv_r.at[i, 3 + d], partner)

    def caches_ready():
        for d in range(NY):
            p = 2 * ((y + NY - d) % NY) + 1 - k
            for i, buf in enumerate((ka, vt)):
                arrive(buf.at[p], kv_r.at[i, 3 + d])

    def pump_first():
        w_second(0)
        w_first(2)

    all_gather(
        0, xb, add_square(xb), send_caches,
        {3: pump_first, 5: lambda: w_third(0)},
    )
    normalise(xb, gain1)
    w_ready(0)
    rows_q = wqf.shape[2] * 2
    acc = jnp.zeros((rows_q, TOK), F32)
    for i in range(NX):
        acc += dot(wqf[i].reshape(rows_q, 1024), nb[8 * i : 8 * i + 8].reshape(1024, TOK))
    gq[y] = acc.astype(BF16)

    for d in (1, 3, 2):
        send(gq.at[y], gq.at[y], q_s.at[d - 1], q_r.at[d - 1], ypeer(d))
    w_second(1)
    w_first(3)
    pass_caches()
    for d in (1, 3, 2):
        arrive(gq.at[(y + NY - d) % NY], q_r.at[d - 1])
    grouped = gq[...].reshape(NY * rows_q, TOK)
    kvn[k] = grouped[4 * HD :]
    send(kvn.at[k], kvn.at[k], q_s.at[3], q_r.at[3], partner)

    def rotate(v, cosine, sine):
        v = v.astype(F32)
        a, b = v[:64], v[64:]
        return jnp.concatenate([a * cosine - b * sine, b * cosine + a * sine], axis=0)

    sn[...] = jnp.zeros_like(sn)
    for head in range(NY):

        @pl.when(y == head)
        def _():
            sn[0] = rotate(grouped[head * HD : (head + 1) * HD], cos[k], sin[k])

    qt = sn[0].astype(BF16)
    length = len_ref[x]
    t_row = lax.broadcasted_iota(jnp.int32, (1, TOK), 1) + TOK * k
    caches_ready()

    def cache_scores(b, peak):
        s = dot(ka[b], qt) * HD ** (-0.5)
        slot = lax.broadcasted_iota(jnp.int32, (SLOTS, 1), 0) + b * SLOTS
        allowed = (slot < length) & (slot > length + t_row - WINDOW)
        s = jnp.where(allowed, s, NEG_FILL)
        sc[b] = s
        return jnp.maximum(peak, jnp.max(s, axis=0, keepdims=True))

    peak = lax.fori_loop(0, WINDOW // SLOTS, cache_scores, jnp.full((1, TOK), NEG_FILL, F32))
    arrive(kvn.at[1 - k], q_r.at[3])
    for h in range(2):
        kt = rotate(kvn[h, :HD], cos[h], sin[h])
        krt[h] = kt.astype(BF16)
        s = dot(jnp.transpose(kt).astype(BF16), qt) * HD ** (-0.5)
        t2 = lax.broadcasted_iota(jnp.int32, (TOK, 1), 0) + TOK * h
        s = jnp.where(t2 <= t_row, s, NEG_FILL)
        sn[h] = s
        peak = jnp.maximum(peak, jnp.max(s, axis=0, keepdims=True))

    def cache_mix(b, carry):
        total, mixed = carry
        e = jnp.exp(sc[b] - peak)
        return (total + jnp.sum(e, axis=0, keepdims=True), mixed + dot(vt[b], e.astype(BF16)))

    total, mixed = lax.fori_loop(
        0, WINDOW // SLOTS, cache_mix, (jnp.zeros((1, TOK), F32), jnp.zeros((HD, TOK), F32))
    )
    for h in range(2):
        e = jnp.exp(sn[h] - peak)
        total = total + jnp.sum(e, axis=0, keepdims=True)
        mixed = mixed + dot(kvn[h, HD:], e.astype(BF16))
    ab[chip] = (mixed / total).astype(BF16)

    def update_caches():
        slot = lax.broadcasted_iota(jnp.int32, (SLOTS, TOK), 0) + (2 * y + k) * SLOTS
        offset = slot - length
        offset = jnp.where(offset < 0, offset + WINDOW, offset)
        lane = lax.broadcasted_iota(jnp.int32, (SLOTS, TOK), 1)
        first = jnp.where(offset == lane, 1.0, 0.0).astype(BF16)
        second = jnp.where(offset == lane + TOK, 1.0, 0.0).astype(BF16)
        fresh = offset < 2 * TOK
        keys = dot_nt(first, krt[0]) + dot_nt(second, krt[1])
        vals = dot_nt(first, kvn[0, HD:]) + dot_nt(second, kvn[1, HD:])
        nk[...] = jnp.where(fresh, keys, kc[...].astype(F32)).astype(BF16)
        nv[...] = jnp.where(fresh, vals, vc[...].astype(F32)).astype(BF16)

    def before_second():
        w_second(2)
        w_first(4)
        w_third(1)
        update_caches()

    all_gather(
        1, ab, lambda c: None, before_second,
        {3: lambda: w_second(3), 5: lambda: w_third(2)},
    )
    w_ready(1)
    rows_o = wof.shape[2] * 2
    acc = xb[chip].astype(F32)
    proj = jnp.zeros((rows_o, TOK), F32)
    for i in range(NX):
        proj += dot(wof[i].reshape(rows_o, 1024), ab[8 * i : 8 * i + 8].reshape(1024, TOK))
    hb[chip] = (acc + proj).astype(BF16)
    ssq[...] = jnp.zeros_like(ssq)

    all_gather(
        2, hb, add_square(hb), lambda: w_second(4),
        {4: lambda: w_third(3)},
    )
    normalise(hb, gain2)
    w_ready(2)
    w_ready(3)
    rows_f = wgf.shape[2] * 2
    gu[...] = jnp.zeros_like(gu)

    def hidden_step(i, carry):
        block = nb[pl.ds(pl.multiple_of(8 * i, 8), 8)].reshape(1024, TOK)
        gu[0] += dot(wgf[i].reshape(rows_f, 1024), block)
        gu[1] += dot(wuf[i].reshape(rows_f, 1024), block)
        return carry

    lax.fori_loop(0, NX, hidden_step, 0)
    gate = gu[0]
    act = (gate / (1.0 + jnp.exp(-gate))) * gu[1]
    act_t = jnp.transpose(act).astype(BF16)
    w_third(4)
    w_ready(4)

    def down(r):
        zz = (z + sg * r + 2 * NZ) % NZ
        cols = pl.ds(pl.multiple_of((zz % 2) * 512, 512), 512)
        part = dot(act_t, wdf[zz // 2, :, :, cols].reshape(rows_f, 512))
        for j in range(NY):
            db[zz * NY + j] = part[:, j * 128 : (j + 1) * 128]

    def plane_row(r, d):
        return ((z + sg * r + 2 * NZ) % NZ) * NY + (y + NY - d) % NY

    def sum_a(s, d):
        v = db[plane_row(5 - s, d)]
        if s > 1:
            arrive(ra.at[s - 2, d], rs_r.at[3 + (s - 2) * 4 + d])
            v = v + ra[s - 2, d].astype(F32)
        sa[s - 1, d] = v.astype(BF16)
        i = 3 + (s - 1) * 4 + d
        send(sa.at[s - 1, d], ra.at[s - 1, d], rs_s.at[i], rs_r.at[i], dev_a)

    def sum_b(s, d):
        v = db[plane_row(s - 4, d)]
        if s > 1:
            arrive(rb.at[s - 2, d], rs_r.at[19 + (s - 2) * 4 + d])
            v = v + rb[s - 2, d].astype(F32)
        sb[s - 1, d] = v.astype(BF16)
        i = 19 + (s - 1) * 4 + d
        send(sb.at[s - 1, d], rb.at[s - 1, d], rs_s.at[i], rs_r.at[i], dev_b)

    down(4)
    for d in (2, 1, 3, 0):
        sum_a(1, d)
    down(-3)
    for d in (2, 1, 3, 0):
        sum_b(1, d)

    def down_step(i, carry):
        down(jnp.where(i % 2 == 0, 3 - i // 2, i // 2 - 2))
        return carry

    lax.fori_loop(0, 6, down_step, 0)
    for s in (2, 3, 4):
        for d in (2, 1, 3, 0):
            sum_a(s, d)
            if s <= 3:
                sum_b(s, d)
    whole = None
    for d in (2, 1, 3, 0):
        arrive(rb.at[2, d], rs_r.at[19 + 8 + d])
        arrive(ra.at[3, d], rs_r.at[3 + 12 + d])
        v = db[plane_row(0, d)] + ra[3, d].astype(F32) + rb[2, d].astype(F32)
        if d == 0:
            whole = v
        else:
            ys[d - 1] = v.astype(BF16)
            send(ys.at[d - 1], yr.at[d - 1], rs_s.at[d - 1], rs_r.at[d - 1], ypeer(NY - d))
    for d in (1, 3, 2):
        arrive(yr.at[d - 1], rs_r.at[d - 1])
        whole = whole + yr[d - 1].astype(F32)
    fin[...] = (hb[chip].astype(F32) + jnp.transpose(whole)).astype(BF16)
    send(fin.at[other_rows], fin_r, rs_s.at[31], rs_r.at[31], partner)
    out[k] = fin[half_rows, :]
    arrive(fin_r, rs_r.at[31])
    out[1 - k] = fin_r[...]
    for copy in pending:
        copy.wait_send()


def per_device(
    hidden_in, cached_len, k_cache, v_cache, attn_gain, ffn_gain, wqkv, wo, wgate, wup, wdown
):
    ht = hidden_in.reshape(2, TOK, 64).transpose(0, 2, 1)
    length = cached_len[lax.axis_index("narrow")]
    exponent = jnp.arange(HD // 2, dtype=F32) * (2.0 / HD)
    frequency = jnp.power(10000.0, -exponent)
    positions = (length + jnp.arange(2 * TOK, dtype=jnp.int32)).astype(F32).reshape(2, 1, TOK)
    angles = positions * frequency[None, :, None]
    gain1 = attn_gain.astype(F32).reshape(CHIPS, 128).T
    gain2 = ffn_gain.astype(F32).reshape(CHIPS, 128).T

    def vm(*shape, dtype=BF16):
        return pltpu.VMEM(shape, dtype)

    def sems(*shape):
        return pltpu.SemaphoreType.DMA(shape)

    def full(w):
        return vm(NX, 2, w.shape[0], w.shape[1])

    in_vmem = pl.BlockSpec(memory_space=pltpu.VMEM)
    in_hbm = pl.BlockSpec(memory_space=pl.ANY)
    out, nk, nv = pl.pallas_call(
        layer_kernel,
        out_shape=(
            jax.ShapeDtypeStruct((2, 64, TOK), BF16),
            jax.ShapeDtypeStruct((SLOTS, HD), BF16),
            jax.ShapeDtypeStruct((SLOTS, HD), BF16),
        ),
        in_specs=[pl.BlockSpec(memory_space=pltpu.SMEM)] + [in_vmem] * 7 + [in_hbm] * 5,
        out_specs=(in_vmem, in_vmem, in_vmem),
        scratch_shapes=[
            vm(CHIPS, 128, TOK), vm(CHIPS, 128, TOK), vm(CHIPS, 128, TOK), vm(CHIPS, 128, TOK),
            vm(NY, 2 * wqkv.shape[0], TOK), vm(2, 2 * HD, TOK), vm(2, HD, TOK),
            vm(8, SLOTS, HD), vm(8, HD, SLOTS),
            vm(8, SLOTS, TOK, dtype=F32), vm(2, TOK, TOK, dtype=F32), vm(8, TOK, dtype=F32),
            full(wqkv), full(wo), full(wgate), full(wup), full(wdown),
            vm(2, 2 * wgate.shape[0], TOK, dtype=F32),
            vm(CHIPS, TOK, 128, dtype=F32),
            vm(4, NY, TOK, 128), vm(3, NY, TOK, 128), vm(4, NY, TOK, 128), vm(3, NY, TOK, 128),
            vm(3, TOK, 128), vm(3, TOK, 128), vm(128, TOK), vm(64, TOK),
            sems(1), sems(1), sems(3, 31), sems(3, 31), sems(5), sems(5, 8), sems(5, 8),
            sems(2, 7), sems(2, 7), sems(4), sems(4), sems(32), sems(32),
        ],
        compiler_params=pltpu.CompilerParams(
            collective_id=0, has_side_effects=True, vmem_limit_bytes=60 * 1024 * 1024
        ),
        name="layer",
    )(
        cached_len, ht, jnp.cos(angles), jnp.sin(angles), gain1, gain2,
        k_cache[0], v_cache[0], wqkv, wo, wgate, wup, wdown,
    )
    hidden_out = out.transpose(0, 2, 1).reshape(2 * TOK, 64)
    return (hidden_out, nk[None], nv[None])


def solution(mesh):
    return jax.shard_map(
        per_device,
        mesh=mesh,
        in_specs=(
            P("narrow", "wide"),
            P(),
            P("narrow", "wide", None),
            P("narrow", "wide", None),
            P(),
            P(),
            P("wide", "narrow"),
            P("wide", "narrow"),
            P("wide", "narrow"),
            P("wide", "narrow"),
            P("wide", "narrow"),
        ),
        out_specs=(P("narrow", "wide"), P("narrow", "wide", None), P("narrow", "wide", None)),
        check_vma=False,
    )
```

```python
import jax
import jax.numpy as jnp
import numpy as np
from jax import lax
from jax.experimental import pallas as pl
from jax.experimental.pallas import tpu as pltpu
from jax.sharding import PartitionSpec as P

HD = 128
WINDOW = 4096
NEG_FILL = -1e30
NZ, NY, NX = 8, 4, 4
CHIPS = NZ * NY
TOK = 128
SLOTS = 512
BF16 = jnp.bfloat16
F32 = jnp.float32
YORDER = (0, 1, 3, 2)
NEAR = (1, -1, 2, -2, 3, -3, 4)
FAR = (4, 3, -3, 2, -2, 1, -1, 0)


def dot(a, b):
    return jnp.dot(a, b, preferred_element_type=F32)


def dot_nt(a, b):
    return lax.dot_general(a, b, (((1,), (1,)), ((), ())), preferred_element_type=F32)


def layer_kernel(
    len_ref, hid, freq, gain1, gain2, kc, vc, wqkv, wo, wg, wu, wd,
    out, nk, nv,
    ht, cos, sin, xb, ab, hb, nb, gq, kvn, krt, ka, vt, sc, sn, ssq,
    wqf, wof, wgf, wuf, wdf, gu, db, ys, yr, zs, zr, fin, fin_r,
    p_s, p_r, ag_s, ag_r, w_l, w_s, w_r, kv_s, kv_r, q_s, q_r, rs_s, rs_r,
):
    wide = lax.axis_index("wide")
    x = lax.axis_index("narrow")
    k = wide % 2
    y = (wide // 2) % NY
    z = wide // (2 * NY)
    sg = 1 - 2 * k
    chip = z * NY + y

    def dev(zz, yy, kk, xx):
        return {"wide": (zz * NY + yy) * 2 + kk, "narrow": xx}

    def ypeer(d):
        return dev(z, (y + d) % NY, k, x)

    def zpeer(d):
        return dev((z + d + NZ) % NZ, y, k, x)

    partner = dev(z, y, 1 - k, x)
    za = (z + sg + NZ) % NZ
    zb = (z - sg + NZ) % NZ
    dev_a = dev(za, y, k, x)
    dev_b = dev(zb, y, k, x)
    xr = (x + 1) % NX
    xl = (x + NX - 1) % NX
    xo = (x + 2) % NX
    dev_xr = dev(z, y, k, xr)
    dev_xl = dev(z, y, k, xl)

    pending = []

    def send(src, dst, s_sem, r_sem, device):
        copy = pltpu.make_async_remote_copy(
            src_ref=src, dst_ref=dst, send_sem=s_sem, recv_sem=r_sem,
            device_id=device, device_id_type=pl.DeviceIdType.MESH,
        )
        copy.start()
        pending.append(copy)

    def arrive(dst, r_sem):
        pltpu.make_async_remote_copy(
            src_ref=dst, dst_ref=dst, send_sem=r_sem, recv_sem=r_sem,
            device_id=partner, device_id_type=pl.DeviceIdType.MESH,
        ).wait_recv()

    barrier = pltpu.get_barrier_semaphore()
    greet = [partner, ypeer(1), ypeer(2), ypeer(3), dev_xr, dev_xl] + [zpeer(d) for d in NEAR]
    for peer in greet:
        pl.semaphore_signal(barrier, inc=1, device_id=peer, device_id_type=pl.DeviceIdType.MESH)
    for h in range(2):
        ht[h] = hid[:, h * TOK : (h + 1) * TOK]
    vt[2 * y + k] = jnp.transpose(vc[...].astype(F32)).astype(BF16)
    ka[2 * y + k] = kc[...]
    ssq[...] = jnp.zeros_like(ssq)
    pl.semaphore_wait(barrier, len(greet))

    own_w = (wqkv, wo, wg, wu, wd)
    full_w = (wqf, wof, wgf, wuf, wdf)
    locals_w = []

    def w_first(m):
        f, o = full_w[m], own_w[m]
        copy = pltpu.make_async_copy(o, f.at[x, k], w_l.at[m])
        copy.start()
        locals_w.append(copy)
        send(o, f.at[x, k], w_s.at[m, 0], w_r.at[m, 0], dev_xr)
        send(o, f.at[x, k], w_s.at[m, 1], w_r.at[m, 1], dev_xl)
        send(o, f.at[x, k], w_s.at[m, 4], w_r.at[m, 4], partner)

    def w_second(m):
        f = full_w[m]
        half = f.shape[2] // 2
        lo, hi = pl.ds(0, half), pl.ds(half, half)
        arrive(f.at[xl, k], w_r.at[m, 0])
        send(f.at[xl, k, lo], f.at[xl, k, lo], w_s.at[m, 2], w_r.at[m, 2], dev_xr)
        send(f.at[xl, k], f.at[xl, k], w_s.at[m, 5], w_r.at[m, 5], partner)
        arrive(f.at[xr, k], w_r.at[m, 1])
        send(f.at[xr, k, hi], f.at[xr, k, hi], w_s.at[m, 3], w_r.at[m, 3], dev_xl)
        send(f.at[xr, k], f.at[xr, k], w_s.at[m, 6], w_r.at[m, 6], partner)

    def w_third(m):
        f = full_w[m]
        half = f.shape[2] // 2
        lo, hi = pl.ds(0, half), pl.ds(half, half)
        arrive(f.at[xo, k, lo], w_r.at[m, 2])
        arrive(f.at[xo, k, hi], w_r.at[m, 3])
        send(f.at[xo, k], f.at[xo, k], w_s.at[m, 7], w_r.at[m, 7], partner)

    def w_ready(m):
        f = full_w[m]
        locals_w[m].wait()
        for i, block in enumerate((x, xl, xr, xo)):
            arrive(f.at[block, 1 - k], w_r.at[m, 4 + i])

    def all_gather(g, buf, on_chunk, extra, pumps):
        send_sem, recv_sem = ag_s.at[g], ag_r.at[g]

        def a_sem(s, d):
            return 3 + (s - 1) * 4 + d

        def b_sem(s, d):
            return 19 + (s - 1) * 4 + d

        def row(zz, d):
            return ((zz + 2 * NZ) % NZ) * NY + (y + NY - d) % NY

        def push_a(s, d):
            ref = buf.at[row(z - sg * (s - 1), d)]
            send(ref, ref, send_sem.at[a_sem(s, d)], recv_sem.at[a_sem(s, d)], dev_a)

        def push_b(s, d):
            ref = buf.at[row(z + sg * (s - 1), d)]
            send(ref, ref, send_sem.at[b_sem(s, d)], recv_sem.at[b_sem(s, d)], dev_b)

        own = buf.at[chip]
        for d in (1, 3, 2):
            send(own, own, send_sem.at[d - 1], recv_sem.at[d - 1], ypeer(d))
        push_a(1, 0)
        push_b(1, 0)
        extra()
        on_chunk(chip)
        for d in YORDER[1:]:
            arrive(buf.at[row(z, d)], recv_sem.at[d - 1])
            push_a(1, d)
            push_b(1, d)
            on_chunk(row(z, d))
        for s in range(2, 6):
            for d in YORDER:
                c = row(z - sg * (s - 1), d)
                arrive(buf.at[c], recv_sem.at[a_sem(s - 1, d)])
                if s <= 4:
                    push_a(s, d)
                on_chunk(c)
                if s <= 4:
                    c = row(z + sg * (s - 1), d)
                    arrive(buf.at[c], recv_sem.at[b_sem(s - 1, d)])
                    if s <= 3:
                        push_b(s, d)
                    on_chunk(c)
            if s in pumps:
                pumps[s]()

    def all_gather_direct(g, buf, on_chunk, extra, pumps):
        send_sem, recv_sem = ag_s.at[g], ag_r.at[g]

        def row(dz, dy):
            return ((z + dz + NZ) % NZ) * NY + (y + dy + NY) % NY

        def y_sem(dz, d):
            return 8 + (dz % NZ) * 3 + d - 1

        def y_send(dz):
            ref = buf.at[row(dz, 0)]
            for d in (2, 1, 3):
                send(ref, ref, send_sem.at[y_sem(dz, d)], recv_sem.at[y_sem(dz, d)], ypeer(d))

        own = buf.at[chip]
        for dz in NEAR:
            send(own, own, send_sem.at[dz % NZ], recv_sem.at[dz % NZ], zpeer(dz))
        y_send(0)
        extra()
        on_chunk(chip)
        for dz in NEAR:
            arrive(buf.at[row(-dz, 0)], recv_sem.at[dz % NZ])
            y_send(-dz)
            on_chunk(row(-dz, 0))
        for i, dz in enumerate((0,) + NEAR):
            for d in (1, 3, 2):
                arrive(buf.at[row(-dz, -d)], recv_sem.at[y_sem(-dz, d)])
                on_chunk(row(-dz, -d))
            if i in pumps:
                pumps[i]()

    def add_square(buf):
        def run(c):
            v = buf[c].astype(F32)
            ssq[...] += jnp.sum((v * v).reshape(16, 8, TOK), axis=0)

        return run

    def normalise(buf, gain):
        mean_square = jnp.sum(ssq[...], axis=0, keepdims=True) * (1.0 / (CHIPS * 128))
        r = lax.rsqrt(mean_square + 1e-05)
        gains = jnp.transpose(gain[...].astype(F32))
        for c in range(CHIPS):
            nb[c] = (buf[c].astype(F32) * r * gains[:, c : c + 1]).astype(BF16)

    half_rows = pl.ds(pl.multiple_of(k * 64, 64), 64)
    other_rows = pl.ds(pl.multiple_of((1 - k) * 64, 64), 64)
    send(ht.at[1 - k], xb.at[chip, half_rows], p_s.at[0], p_r.at[0], partner)
    xb[chip, half_rows, :] = ht[k]
    w_first(0)
    w_first(1)
    arrive(xb.at[chip, other_rows], p_r.at[0])

    def send_caches():
        p = 2 * y + k
        for d in (1, 3, 2):
            send(ka.at[p], ka.at[p], kv_s.at[0, d - 1], kv_r.at[0, d - 1], ypeer(d))
            send(vt.at[p], vt.at[p], kv_s.at[1, d - 1], kv_r.at[1, d - 1], ypeer(d))
        send(ka.at[p], ka.at[p], kv_s.at[0, 3], kv_r.at[0, 3], partner)
        send(vt.at[p], vt.at[p], kv_s.at[1, 3], kv_r.at[1, 3], partner)

    def pass_caches():
        for d in (1, 3, 2):
            p = 2 * ((y + NY - d) % NY) + k
            for i, buf in enumerate((ka, vt)):
                arrive(buf.at[p], kv_r.at[i, d - 1])
                send(buf.at[p], buf.at[p], kv_s.at[i, 3 + d], kv_r.at[i, 3 + d], partner)

    def caches_ready():
        for d in range(NY):
            p = 2 * ((y + NY - d) % NY) + 1 - k
            for i, buf in enumerate((ka, vt)):
                arrive(buf.at[p], kv_r.at[i, 3 + d])

    def before_first():
        send_caches()
        for h in range(2):
            t = lax.broadcasted_iota(jnp.int32, (1, TOK), 1) + (TOK * h + len_ref[x])
            angle = freq[:, 0:1] * t.astype(F32)
            cos[h] = jnp.cos(angle)
            sin[h] = jnp.sin(angle)

    def pump_first():
        w_second(0)
        w_first(2)

    all_gather(
        0, xb, add_square(xb), before_first,
        {3: pump_first, 5: lambda: w_third(0)},
    )
    normalise(xb, gain1)
    w_ready(0)
    rows_q = wqf.shape[2] * 2
    acc = jnp.zeros((rows_q, TOK), F32)
    for i in range(NX):
        acc += dot(wqf[i].reshape(rows_q, 1024), nb[8 * i : 8 * i + 8].reshape(1024, TOK))
    gq[y] = acc.astype(BF16)

    for d in (1, 3, 2):
        send(gq.at[y], gq.at[y], q_s.at[d - 1], q_r.at[d - 1], ypeer(d))
    w_second(1)
    w_first(3)
    pass_caches()
    for d in (1, 3, 2):
        arrive(gq.at[(y + NY - d) % NY], q_r.at[d - 1])
    grouped = gq[...].reshape(NY * rows_q, TOK)
    kvn[k] = grouped[4 * HD :]
    send(kvn.at[k], kvn.at[k], q_s.at[3], q_r.at[3], partner)

    def rotate(v, cosine, sine):
        v = v.astype(F32)
        a, b = v[:64], v[64:]
        return jnp.concatenate([a * cosine - b * sine, b * cosine + a * sine], axis=0)

    sn[...] = jnp.zeros_like(sn)
    for head in range(NY):

        @pl.when(y == head)
        def _():
            sn[0] = rotate(grouped[head * HD : (head + 1) * HD], cos[k], sin[k])

    qt = sn[0].astype(BF16)
    length = len_ref[x]
    t_row = lax.broadcasted_iota(jnp.int32, (1, TOK), 1) + TOK * k
    caches_ready()

    def cache_scores(b, peak):
        s = dot(ka[b], qt) * HD ** (-0.5)
        slot = lax.broadcasted_iota(jnp.int32, (SLOTS, 1), 0) + b * SLOTS
        allowed = (slot < length) & (slot > length + t_row - WINDOW)
        s = jnp.where(allowed, s, NEG_FILL)
        sc[b] = s
        return jnp.maximum(peak, jnp.max(s, axis=0, keepdims=True))

    peak = lax.fori_loop(0, WINDOW // SLOTS, cache_scores, jnp.full((1, TOK), NEG_FILL, F32))
    arrive(kvn.at[1 - k], q_r.at[3])
    for h in range(2):
        kt = rotate(kvn[h, :HD], cos[h], sin[h])
        krt[h] = kt.astype(BF16)
        s = dot(jnp.transpose(kt).astype(BF16), qt) * HD ** (-0.5)
        t2 = lax.broadcasted_iota(jnp.int32, (TOK, 1), 0) + TOK * h
        s = jnp.where(t2 <= t_row, s, NEG_FILL)
        sn[h] = s
        peak = jnp.maximum(peak, jnp.max(s, axis=0, keepdims=True))

    def cache_mix(b, carry):
        total, mixed = carry
        e = jnp.exp(sc[b] - peak)
        return (total + jnp.sum(e, axis=0, keepdims=True), mixed + dot(vt[b], e.astype(BF16)))

    total, mixed = lax.fori_loop(
        0, WINDOW // SLOTS, cache_mix, (jnp.zeros((1, TOK), F32), jnp.zeros((HD, TOK), F32))
    )
    for h in range(2):
        e = jnp.exp(sn[h] - peak)
        total = total + jnp.sum(e, axis=0, keepdims=True)
        mixed = mixed + dot(kvn[h, HD:], e.astype(BF16))
    ab[chip] = (mixed / total).astype(BF16)

    def update_caches():
        slot = lax.broadcasted_iota(jnp.int32, (SLOTS, TOK), 0) + (2 * y + k) * SLOTS
        offset = slot - length
        offset = jnp.where(offset < 0, offset + WINDOW, offset)
        lane = lax.broadcasted_iota(jnp.int32, (SLOTS, TOK), 1)
        first = jnp.where(offset == lane, 1.0, 0.0).astype(BF16)
        second = jnp.where(offset == lane + TOK, 1.0, 0.0).astype(BF16)
        fresh = offset < 2 * TOK
        keys = dot_nt(first, krt[0]) + dot_nt(second, krt[1])
        vals = dot_nt(first, kvn[0, HD:]) + dot_nt(second, kvn[1, HD:])
        nk[...] = jnp.where(fresh, keys, kc[...].astype(F32)).astype(BF16)
        nv[...] = jnp.where(fresh, vals, vc[...].astype(F32)).astype(BF16)

    def before_second():
        w_second(2)
        w_first(4)
        w_third(1)
        update_caches()

    all_gather_direct(
        1, ab, lambda c: None, before_second,
        {4: lambda: w_second(3), 7: lambda: w_third(2)},
    )
    w_ready(1)
    rows_o = wof.shape[2] * 2
    acc = xb[chip].astype(F32)
    proj = jnp.zeros((rows_o, TOK), F32)
    for i in range(NX):
        proj += dot(wof[i].reshape(rows_o, 1024), ab[8 * i : 8 * i + 8].reshape(1024, TOK))
    hb[chip] = (acc + proj).astype(BF16)
    ssq[...] = jnp.zeros_like(ssq)

    all_gather_direct(
        2, hb, add_square(hb), lambda: None,
        {3: lambda: w_second(4), 7: lambda: w_third(3)},
    )
    normalise(hb, gain2)
    w_ready(2)
    w_ready(3)
    rows_f = wgf.shape[2] * 2
    gu[...] = jnp.zeros_like(gu)

    def hidden_step(i, carry):
        block = nb[pl.ds(pl.multiple_of(8 * i, 8), 8)].reshape(1024, TOK)
        gu[0] += dot(wgf[i].reshape(rows_f, 1024), block)
        gu[1] += dot(wuf[i].reshape(rows_f, 1024), block)
        return carry

    lax.fori_loop(0, NX, hidden_step, 0)
    gate = gu[0]
    act = (gate / (1.0 + jnp.exp(-gate))) * gu[1]
    act_t = jnp.transpose(act).astype(BF16)
    w_third(4)
    w_ready(4)

    for i, r in enumerate(FAR):
        zz = (z + r + NZ) % NZ
        cols = pl.ds(pl.multiple_of((zz % 2) * 512, 512), 512)
        db[i] = dot(act_t, wdf[zz // 2, :, :, cols].reshape(rows_f, 512))
        for d in (2, 1, 3):
            col = pl.ds(pl.multiple_of(((y + d) % NY) * 128, 128), 128)
            ys[i, d - 1] = db[i, :, col].astype(BF16)
            n = 3 * i + d - 1
            send(ys.at[i, d - 1], yr.at[i, d - 1], rs_s.at[n], rs_r.at[n], ypeer(d))
    own_col = pl.ds(pl.multiple_of(y * 128, 128), 128)
    whole = None
    for i, r in enumerate(FAR):
        v = db[i, :, own_col]
        for d in (1, 3, 2):
            arrive(yr.at[i, d - 1], rs_r.at[3 * i + d - 1])
            v = v + yr[i, d - 1].astype(F32)
        if r == 0:
            whole = v
        else:
            zs[i] = v.astype(BF16)
            send(zs.at[i], zr.at[i], rs_s.at[24 + i], rs_r.at[24 + i], zpeer(r))
    for i in reversed(range(NZ - 1)):
        arrive(zr.at[i], rs_r.at[24 + i])
        whole = whole + zr[i].astype(F32)
    fin[...] = (hb[chip].astype(F32) + jnp.transpose(whole)).astype(BF16)
    send(fin.at[other_rows], fin_r, rs_s.at[31], rs_r.at[31], partner)
    out[:, pl.ds(pl.multiple_of(k * TOK, TOK), TOK)] = fin[half_rows, :]
    arrive(fin_r, rs_r.at[31])
    out[:, pl.ds(pl.multiple_of((1 - k) * TOK, TOK), TOK)] = fin_r[...]
    for copy in pending:
        copy.wait_send()


def per_device(
    hidden_in, cached_len, k_cache, v_cache, attn_gain, ffn_gain, wqkv, wo, wgate, wup, wdown
):
    exponent = np.arange(HD // 2, dtype=np.float32) * np.float32(2.0 / HD)
    frequency = np.power(np.float32(10000.0), -exponent).astype(np.float32)
    freq = jnp.asarray(np.outer(frequency, np.arange(1, TOK + 1, dtype=np.float32)))

    def vm(*shape, dtype=BF16):
        return pltpu.VMEM(shape, dtype)

    def sems(*shape):
        return pltpu.SemaphoreType.DMA(shape)

    def full(w):
        return vm(NX, 2, w.shape[0], w.shape[1])

    in_vmem = pl.BlockSpec(memory_space=pltpu.VMEM)
    in_hbm = pl.BlockSpec(memory_space=pl.ANY)
    out, nk, nv = pl.pallas_call(
        layer_kernel,
        out_shape=(
            jax.ShapeDtypeStruct((64, 2 * TOK), BF16),
            jax.ShapeDtypeStruct((SLOTS, HD), BF16),
            jax.ShapeDtypeStruct((SLOTS, HD), BF16),
        ),
        in_specs=[pl.BlockSpec(memory_space=pltpu.SMEM)] + [in_vmem] * 6 + [in_hbm] * 5,
        out_specs=(in_vmem, in_vmem, in_vmem),
        scratch_shapes=[
            vm(2, 64, TOK), vm(2, 64, TOK, dtype=F32), vm(2, 64, TOK, dtype=F32),
            vm(CHIPS, 128, TOK), vm(CHIPS, 128, TOK), vm(CHIPS, 128, TOK), vm(CHIPS, 128, TOK),
            vm(NY, 2 * wqkv.shape[0], TOK), vm(2, 2 * HD, TOK), vm(2, HD, TOK),
            vm(8, SLOTS, HD), vm(8, HD, SLOTS),
            vm(8, SLOTS, TOK, dtype=F32), vm(2, TOK, TOK, dtype=F32), vm(8, TOK, dtype=F32),
            full(wqkv), full(wo), full(wgate), full(wup), full(wdown),
            vm(2, 2 * wgate.shape[0], TOK, dtype=F32),
            vm(NZ, TOK, 512, dtype=F32),
            vm(NZ, 3, TOK, 128), vm(NZ, 3, TOK, 128), vm(NZ - 1, TOK, 128), vm(NZ - 1, TOK, 128),
            vm(128, TOK), vm(64, TOK),
            sems(1), sems(1), sems(3, 32), sems(3, 32), sems(5), sems(5, 8), sems(5, 8),
            sems(2, 7), sems(2, 7), sems(4), sems(4), sems(32), sems(32),
        ],
        compiler_params=pltpu.CompilerParams(
            collective_id=0, has_side_effects=True, vmem_limit_bytes=60 * 1024 * 1024
        ),
        name="layer",
    )(
        cached_len, hidden_in.T, freq, attn_gain.reshape(CHIPS, 128), ffn_gain.reshape(CHIPS, 128),
        k_cache[0], v_cache[0], wqkv, wo, wgate, wup, wdown,
    )
    return (out.T, nk[None], nv[None])


def solution(mesh):
    return jax.shard_map(
        per_device,
        mesh=mesh,
        in_specs=(
            P("narrow", "wide"),
            P(),
            P("narrow", "wide", None),
            P("narrow", "wide", None),
            P(),
            P(),
            P("wide", "narrow"),
            P("wide", "narrow"),
            P("wide", "narrow"),
            P("wide", "narrow"),
            P("wide", "narrow"),
        ),
        out_specs=(P("narrow", "wide"), P("narrow", "wide", None), P("narrow", "wide", None)),
        check_vma=False,
    )
```

```python
import jax
import jax.numpy as jnp
import numpy as np
from jax import lax
from jax.experimental import pallas as pl
from jax.experimental.pallas import tpu as pltpu
from jax.sharding import PartitionSpec as P

HD = 128
WINDOW = 4096
NEG_FILL = -1e30
NZ, NY, NX = 8, 4, 4
CHIPS = NZ * NY
TOK = 128
SLOTS = 512
BF16 = jnp.bfloat16
F32 = jnp.float32
YORDER = (0, 1, 3, 2)
NEAR = (1, -1, 2, -2, 3, -3, 4)


def dot(a, b):
    return jnp.dot(a, b, preferred_element_type=F32)


def dot_nt(a, b):
    return lax.dot_general(a, b, (((1,), (1,)), ((), ())), preferred_element_type=F32)


def layer_kernel(
    len_ref, hid, freq, gain1, gain2, kc, vc, wqkv, wo, wg, wu, wd,
    out, new_k, new_v,
    ht, cos, sin, xb, ab, hb, nb, gq, kvn, krt, ka, vt, sc, sn, ssq,
    wqf, wof, wgf, wuf, wdf, gu, db, total_f, ys, yr, zs, zr, fin, fin_r,
    p_s, p_r, ag_s, ag_r, w_l, w_s, w_r, kv_s, kv_r, q_s, q_r, rs_s, rs_r,
):
    wide = lax.axis_index("wide")
    x = lax.axis_index("narrow")
    k = wide % 2
    y = (wide // 2) % NY
    z = wide // (2 * NY)
    sg = 1 - 2 * k
    chip = z * NY + y

    def dev(zz, yy, kk, xx):
        return {"wide": (zz * NY + yy) * 2 + kk, "narrow": xx}

    def ypeer(d):
        return dev(z, (y + d) % NY, k, x)

    def zpeer(d):
        return dev((z + d + NZ) % NZ, y, k, x)

    partner = dev(z, y, 1 - k, x)
    za = (z + sg + NZ) % NZ
    zb = (z - sg + NZ) % NZ
    dev_a = dev(za, y, k, x)
    dev_b = dev(zb, y, k, x)
    xr = (x + 1) % NX
    xl = (x + NX - 1) % NX
    xo = (x + 2) % NX
    dev_xr = dev(z, y, k, xr)
    dev_xl = dev(z, y, k, xl)

    pending = []

    def send(src, dst, s_sem, r_sem, device):
        copy = pltpu.make_async_remote_copy(
            src_ref=src, dst_ref=dst, send_sem=s_sem, recv_sem=r_sem,
            device_id=device, device_id_type=pl.DeviceIdType.MESH,
        )
        copy.start()
        pending.append(copy)

    def arrive(dst, r_sem):
        pltpu.make_async_remote_copy(
            src_ref=dst, dst_ref=dst, send_sem=r_sem, recv_sem=r_sem,
            device_id=partner, device_id_type=pl.DeviceIdType.MESH,
        ).wait_recv()

    barrier = pltpu.get_barrier_semaphore()
    greet = [partner, ypeer(1), ypeer(2), ypeer(3), dev_xr, dev_xl] + [zpeer(d) for d in NEAR]
    for peer in greet:
        pl.semaphore_signal(barrier, inc=1, device_id=peer, device_id_type=pl.DeviceIdType.MESH)
    for h in range(2):
        ht[h] = hid[:, h * TOK : (h + 1) * TOK]
    vt[2 * y + k] = jnp.transpose(vc[...].astype(F32)).astype(BF16)
    ka[2 * y + k] = kc[...]
    ssq[...] = jnp.zeros_like(ssq)
    pl.semaphore_wait(barrier, len(greet))

    own_w = (wqkv, wo, wg, wu, wd)
    full_w = (wqf, wof, wgf, wuf, wdf)
    locals_w = []

    def w_first(m):
        f, o = full_w[m], own_w[m]
        copy = pltpu.make_async_copy(o, f.at[x, k], w_l.at[m])
        copy.start()
        locals_w.append(copy)
        send(o, f.at[x, k], w_s.at[m, 0], w_r.at[m, 0], dev_xr)
        send(o, f.at[x, k], w_s.at[m, 1], w_r.at[m, 1], dev_xl)
        send(o, f.at[x, k], w_s.at[m, 4], w_r.at[m, 4], partner)

    def w_second(m):
        f = full_w[m]
        half = f.shape[2] // 2
        lo, hi = pl.ds(0, half), pl.ds(half, half)
        arrive(f.at[xl, k], w_r.at[m, 0])
        send(f.at[xl, k, lo], f.at[xl, k, lo], w_s.at[m, 2], w_r.at[m, 2], dev_xr)
        send(f.at[xl, k], f.at[xl, k], w_s.at[m, 5], w_r.at[m, 5], partner)
        arrive(f.at[xr, k], w_r.at[m, 1])
        send(f.at[xr, k, hi], f.at[xr, k, hi], w_s.at[m, 3], w_r.at[m, 3], dev_xl)
        send(f.at[xr, k], f.at[xr, k], w_s.at[m, 6], w_r.at[m, 6], partner)

    def w_third(m):
        f = full_w[m]
        half = f.shape[2] // 2
        lo, hi = pl.ds(0, half), pl.ds(half, half)
        arrive(f.at[xo, k, lo], w_r.at[m, 2])
        arrive(f.at[xo, k, hi], w_r.at[m, 3])
        send(f.at[xo, k], f.at[xo, k], w_s.at[m, 7], w_r.at[m, 7], partner)

    blocks = (x, xl, xr, xo)

    def w_ready(m, i):
        if i == 0:
            locals_w[m].wait()
        arrive(full_w[m].at[blocks[i], 1 - k], w_r.at[m, 4 + i])

    def rows_of(buf, i):
        return buf[pl.ds(pl.multiple_of(8 * blocks[i], 8), 8)].reshape(1024, TOK)

    def all_gather(g, buf, on_chunk, extra, pumps):
        send_sem, recv_sem = ag_s.at[g], ag_r.at[g]

        def a_sem(s, d):
            return 3 + (s - 1) * 4 + d

        def b_sem(s, d):
            return 19 + (s - 1) * 4 + d

        def row(zz, d):
            return ((zz + 2 * NZ) % NZ) * NY + (y + NY - d) % NY

        def push_a(s, d):
            ref = buf.at[row(z - sg * (s - 1), d)]
            send(ref, ref, send_sem.at[a_sem(s, d)], recv_sem.at[a_sem(s, d)], dev_a)

        def push_b(s, d):
            ref = buf.at[row(z + sg * (s - 1), d)]
            send(ref, ref, send_sem.at[b_sem(s, d)], recv_sem.at[b_sem(s, d)], dev_b)

        own = buf.at[chip]
        for d in (1, 3, 2):
            send(own, own, send_sem.at[d - 1], recv_sem.at[d - 1], ypeer(d))
        push_a(1, 0)
        push_b(1, 0)
        extra()
        on_chunk(chip)
        for d in YORDER[1:]:
            arrive(buf.at[row(z, d)], recv_sem.at[d - 1])
            push_a(1, d)
            push_b(1, d)
            on_chunk(row(z, d))
        for s in range(2, 6):
            for d in YORDER:
                c = row(z - sg * (s - 1), d)
                arrive(buf.at[c], recv_sem.at[a_sem(s - 1, d)])
                if s <= 4:
                    push_a(s, d)
                on_chunk(c)
                if s <= 4:
                    c = row(z + sg * (s - 1), d)
                    arrive(buf.at[c], recv_sem.at[b_sem(s - 1, d)])
                    if s <= 3:
                        push_b(s, d)
                    on_chunk(c)
                if (s, d) in pumps:
                    pumps[s, d]()

    def all_gather_direct(g, buf, on_chunk, extra, pumps):
        send_sem, recv_sem = ag_s.at[g], ag_r.at[g]

        def row(dz, dy):
            return ((z + dz + NZ) % NZ) * NY + (y + dy + NY) % NY

        def y_sem(dz, d):
            return 8 + (dz % NZ) * 3 + d - 1

        def y_send(dz):
            ref = buf.at[row(dz, 0)]
            for d in (2, 1, 3):
                send(ref, ref, send_sem.at[y_sem(dz, d)], recv_sem.at[y_sem(dz, d)], ypeer(d))

        own = buf.at[chip]
        for dz in NEAR:
            send(own, own, send_sem.at[dz % NZ], recv_sem.at[dz % NZ], zpeer(dz))
        y_send(0)
        extra()
        on_chunk(chip)
        for dz in NEAR:
            arrive(buf.at[row(-dz, 0)], recv_sem.at[dz % NZ])
            y_send(-dz)
            on_chunk(row(-dz, 0))
        for i, dz in enumerate((0,) + NEAR):
            for d in (1, 3, 2):
                arrive(buf.at[row(-dz, -d)], recv_sem.at[y_sem(-dz, d)])
                on_chunk(row(-dz, -d))
            if i in pumps:
                pumps[i]()

    def add_square(buf):
        def run(c):
            v = buf[c].astype(F32)
            ssq[...] += jnp.sum((v * v).reshape(16, 8, TOK), axis=0)

        return run

    def normalise(buf, gain):
        mean_square = jnp.sum(ssq[...], axis=0, keepdims=True) * (1.0 / (CHIPS * 128))
        r = lax.rsqrt(mean_square + 1e-05)
        gains = jnp.transpose(gain[...].astype(F32))
        for c in range(CHIPS):
            nb[c] = (buf[c].astype(F32) * r * gains[:, c : c + 1]).astype(BF16)

    half_rows = pl.ds(pl.multiple_of(k * 64, 64), 64)
    other_rows = pl.ds(pl.multiple_of((1 - k) * 64, 64), 64)
    send(ht.at[1 - k], xb.at[chip, half_rows], p_s.at[0], p_r.at[0], partner)
    xb[chip, half_rows, :] = ht[k]
    w_first(0)
    w_first(1)
    arrive(xb.at[chip, other_rows], p_r.at[0])

    def send_caches():
        p = 2 * y + k
        for d in (1, 3, 2):
            send(ka.at[p], ka.at[p], kv_s.at[0, d - 1], kv_r.at[0, d - 1], ypeer(d))
            send(vt.at[p], vt.at[p], kv_s.at[1, d - 1], kv_r.at[1, d - 1], ypeer(d))
        send(ka.at[p], ka.at[p], kv_s.at[0, 3], kv_r.at[0, 3], partner)
        send(vt.at[p], vt.at[p], kv_s.at[1, 3], kv_r.at[1, 3], partner)

    def pass_caches():
        for d in (1, 3, 2):
            p = 2 * ((y + NY - d) % NY) + k
            for i, buf in enumerate((ka, vt)):
                arrive(buf.at[p], kv_r.at[i, d - 1])
                send(buf.at[p], buf.at[p], kv_s.at[i, 3 + d], kv_r.at[i, 3 + d], partner)

    def caches_ready():
        for d in range(NY):
            p = 2 * ((y + NY - d) % NY) + 1 - k
            for i, buf in enumerate((ka, vt)):
                arrive(buf.at[p], kv_r.at[i, 3 + d])

    def before_first():
        send_caches()
        for h in range(2):
            t = lax.broadcasted_iota(jnp.int32, (1, TOK), 1) + (TOK * h + len_ref[x])
            angle = freq[:, 0:1] * t.astype(F32)
            cos[h] = jnp.cos(angle)
            sin[h] = jnp.sin(angle)

    def pump_first():
        w_second(0)
        w_first(2)

    def pump_second():
        w_second(1)
        w_first(3)

    def pump_third():
        w_third(0)
        w_first(4)

    all_gather(
        0, xb, add_square(xb), before_first,
        {(2, 2): pump_first, (3, 2): pump_second, (5, 1): pump_third},
    )
    normalise(xb, gain1)
    rows_q = wqf.shape[2] * 2
    acc = jnp.zeros((rows_q, TOK), F32)
    for i in range(NX):
        w_ready(0, i)
        acc += dot(wqf[blocks[i]].reshape(rows_q, 1024), rows_of(nb, i))
    gq[y] = acc.astype(BF16)

    for d in (1, 3, 2):
        send(gq.at[y], gq.at[y], q_s.at[d - 1], q_r.at[d - 1], ypeer(d))
    pass_caches()
    for d in (1, 3, 2):
        arrive(gq.at[(y + NY - d) % NY], q_r.at[d - 1])
    grouped = gq[...].reshape(NY * rows_q, TOK)
    kvn[k] = grouped[4 * HD :]
    send(kvn.at[k], kvn.at[k], q_s.at[3], q_r.at[3], partner)

    def rotate(v, cosine, sine):
        v = v.astype(F32)
        a, b = v[:64], v[64:]
        return jnp.concatenate([a * cosine - b * sine, b * cosine + a * sine], axis=0)

    sn[...] = jnp.zeros_like(sn)
    for head in range(NY):

        @pl.when(y == head)
        def _():
            sn[0] = rotate(grouped[head * HD : (head + 1) * HD], cos[k], sin[k])

    qt = sn[0].astype(BF16)
    length = len_ref[x]
    t_row = lax.broadcasted_iota(jnp.int32, (1, TOK), 1) + TOK * k
    caches_ready()

    def cache_scores(b, peak):
        s = dot(ka[b], qt) * HD ** (-0.5)
        slot = lax.broadcasted_iota(jnp.int32, (SLOTS, 1), 0) + b * SLOTS
        allowed = (slot < length) & (slot > length + t_row - WINDOW)
        s = jnp.where(allowed, s, NEG_FILL)
        sc[b] = s
        return jnp.maximum(peak, jnp.max(s, axis=0, keepdims=True))

    peak = lax.fori_loop(0, WINDOW // SLOTS, cache_scores, jnp.full((1, TOK), NEG_FILL, F32))
    arrive(kvn.at[1 - k], q_r.at[3])
    for h in range(2):
        kt = rotate(kvn[h, :HD], cos[h], sin[h])
        krt[h] = kt.astype(BF16)
        s = dot(jnp.transpose(kt).astype(BF16), qt) * HD ** (-0.5)
        t2 = lax.broadcasted_iota(jnp.int32, (TOK, 1), 0) + TOK * h
        s = jnp.where(t2 <= t_row, s, NEG_FILL)
        sn[h] = s
        peak = jnp.maximum(peak, jnp.max(s, axis=0, keepdims=True))

    def cache_mix(b, carry):
        total, mixed = carry
        e = jnp.exp(sc[b] - peak)
        return (total + jnp.sum(e, axis=0, keepdims=True), mixed + dot(vt[b], e.astype(BF16)))

    total, mixed = lax.fori_loop(
        0, WINDOW // SLOTS, cache_mix, (jnp.zeros((1, TOK), F32), jnp.zeros((HD, TOK), F32))
    )
    for h in range(2):
        e = jnp.exp(sn[h] - peak)
        total = total + jnp.sum(e, axis=0, keepdims=True)
        mixed = mixed + dot(kvn[h, HD:], e.astype(BF16))
    ab[chip] = (mixed / total).astype(BF16)

    def before_second():
        w_second(2)
        w_third(1)
        for h in range(2):
            new_k[h] = krt[h]
            new_v[h] = kvn[h, HD:]

    all_gather_direct(
        1, ab, lambda c: None, before_second,
        {4: lambda: w_second(3)},
    )
    rows_o = wof.shape[2] * 2
    acc = xb[chip].astype(F32)
    proj = jnp.zeros((rows_o, TOK), F32)
    for i in range(NX):
        w_ready(1, i)
        proj += dot(wof[blocks[i]].reshape(rows_o, 1024), rows_of(ab, i))
    hb[chip] = (acc + proj).astype(BF16)
    ssq[...] = jnp.zeros_like(ssq)

    all_gather_direct(
        2, hb, add_square(hb), lambda: None,
        {0: lambda: w_second(4), 4: lambda: w_third(2), 7: lambda: w_third(3)},
    )
    normalise(hb, gain2)
    rows_f = wgf.shape[2] * 2
    for i in range(NX):
        block = rows_of(nb, i)
        for m, f in ((2, wgf), (3, wuf)):
            w_ready(m, i)
            part = dot(f[blocks[i]].reshape(rows_f, 1024), block)
            gu[m - 2] = part if i == 0 else gu[m - 2] + part
    gate = gu[0]
    act = (gate / (1.0 + jnp.exp(-gate))) * gu[1]
    act_t = jnp.transpose(act).astype(BF16)

    for i in range(NZ):
        block = blocks[i // 2]
        if i == 4:
            w_third(4)
        if i % 2 == 0:
            w_ready(4, i // 2)
        cols = pl.ds((i % 2) * 512, 512)
        db[i] = dot(act_t, wdf[block, :, :, cols].reshape(rows_f, 512))
        for d in (2, 1, 3):
            col = pl.ds(pl.multiple_of(((y + d) % NY) * 128, 128), 128)
            ys[i, d - 1] = db[i, :, col].astype(BF16)
            n = 3 * i + d - 1
            send(ys.at[i, d - 1], yr.at[i, d - 1], rs_s.at[n], rs_r.at[n], ypeer(d))
    own_col = pl.ds(pl.multiple_of(y * 128, 128), 128)
    for i in range(NZ):
        zz = 2 * blocks[i // 2] + i % 2
        disp = (zz - z + NZ) % NZ
        v = db[i, :, own_col]
        for d in (1, 3, 2):
            arrive(yr.at[i, d - 1], rs_r.at[3 * i + d - 1])
            v = v + yr[i, d - 1].astype(F32)
        zs[disp] = v.astype(BF16)

        @pl.when(disp == 0)
        def _():
            total_f[...] = v

        @pl.when(disp != 0)
        def _():
            pltpu.make_async_remote_copy(
                src_ref=zs.at[disp], dst_ref=zr.at[disp],
                send_sem=rs_s.at[23 + disp], recv_sem=rs_r.at[23 + disp],
                device_id=dev(zz, y, k, x), device_id_type=pl.DeviceIdType.MESH,
            ).start()

    whole = total_f[...]
    for dz in NEAR:
        arrive(zr.at[dz % NZ], rs_r.at[23 + dz % NZ])
        whole = whole + zr[dz % NZ].astype(F32)
    fin[...] = (hb[chip].astype(F32) + jnp.transpose(whole)).astype(BF16)
    send(fin.at[other_rows], fin_r, rs_s.at[31], rs_r.at[31], partner)
    out[:, pl.ds(pl.multiple_of(k * TOK, TOK), TOK)] = fin[half_rows, :]
    arrive(fin_r, rs_r.at[31])
    out[:, pl.ds(pl.multiple_of((1 - k) * TOK, TOK), TOK)] = fin_r[...]
    for copy in pending:
        copy.wait_send()
    for i in range(1, NZ):
        pltpu.make_async_remote_copy(
            src_ref=zs.at[i], dst_ref=zr.at[i], send_sem=rs_s.at[23 + i], recv_sem=rs_r.at[23 + i],
            device_id=partner, device_id_type=pl.DeviceIdType.MESH,
        ).wait_send()


def cache_kernel(len_ref, hid, new_k, new_v, kc, vc, out, nk, nv):
    length = len_ref[lax.axis_index("narrow")]
    slot = lax.broadcasted_iota(jnp.int32, (SLOTS, TOK), 0) + lax.axis_index("wide") % 8 * SLOTS
    offset = slot - length
    offset = jnp.where(offset < 0, offset + WINDOW, offset)
    lane = lax.broadcasted_iota(jnp.int32, (SLOTS, TOK), 1)
    first = jnp.where(offset == lane, 1.0, 0.0).astype(BF16)
    second = jnp.where(offset == lane + TOK, 1.0, 0.0).astype(BF16)
    fresh = offset < 2 * TOK
    keys = dot_nt(first, new_k[0]) + dot_nt(second, new_k[1])
    vals = dot_nt(first, new_v[0]) + dot_nt(second, new_v[1])
    nk[...] = jnp.where(fresh, keys, kc[...].astype(F32)).astype(BF16)
    nv[...] = jnp.where(fresh, vals, vc[...].astype(F32)).astype(BF16)
    out[...] = hid[...]


def per_device(
    hidden_in, cached_len, k_cache, v_cache, attn_gain, ffn_gain, wqkv, wo, wgate, wup, wdown
):
    exponent = np.arange(HD // 2, dtype=np.float32) * np.float32(2.0 / HD)
    frequency = np.power(np.float32(10000.0), -exponent).astype(np.float32)
    freq = jnp.asarray(np.outer(frequency, np.arange(1, TOK + 1, dtype=np.float32)))

    def vm(*shape, dtype=BF16):
        return pltpu.VMEM(shape, dtype)

    def sems(*shape):
        return pltpu.SemaphoreType.DMA(shape)

    def full(w):
        return vm(NX, 2, w.shape[0], w.shape[1])

    in_vmem = pl.BlockSpec(memory_space=pltpu.VMEM)
    in_hbm = pl.BlockSpec(memory_space=pl.ANY)
    out, new_k, new_v = pl.pallas_call(
        layer_kernel,
        out_shape=(
            jax.ShapeDtypeStruct((64, 2 * TOK), BF16),
            jax.ShapeDtypeStruct((2, HD, TOK), BF16),
            jax.ShapeDtypeStruct((2, HD, TOK), BF16),
        ),
        in_specs=[pl.BlockSpec(memory_space=pltpu.SMEM)] + [in_vmem] * 6 + [in_hbm] * 5,
        out_specs=(in_vmem, in_vmem, in_vmem),
        scratch_shapes=[
            vm(2, 64, TOK), vm(2, 64, TOK, dtype=F32), vm(2, 64, TOK, dtype=F32),
            vm(CHIPS, 128, TOK), vm(CHIPS, 128, TOK), vm(CHIPS, 128, TOK), vm(CHIPS, 128, TOK),
            vm(NY, 2 * wqkv.shape[0], TOK), vm(2, 2 * HD, TOK), vm(2, HD, TOK),
            vm(8, SLOTS, HD), vm(8, HD, SLOTS),
            vm(8, SLOTS, TOK, dtype=F32), vm(2, TOK, TOK, dtype=F32), vm(8, TOK, dtype=F32),
            full(wqkv), full(wo), full(wgate), full(wup), full(wdown),
            vm(2, 2 * wgate.shape[0], TOK, dtype=F32),
            vm(NZ, TOK, 512, dtype=F32), vm(TOK, 128, dtype=F32),
            vm(NZ, 3, TOK, 128), vm(NZ, 3, TOK, 128), vm(NZ, TOK, 128), vm(NZ, TOK, 128),
            vm(128, TOK), vm(64, TOK),
            sems(1), sems(1), sems(3, 32), sems(3, 32), sems(5), sems(5, 8), sems(5, 8),
            sems(2, 7), sems(2, 7), sems(4), sems(4), sems(32), sems(32),
        ],
        compiler_params=pltpu.CompilerParams(
            collective_id=0, has_side_effects=True, vmem_limit_bytes=60 * 1024 * 1024
        ),
        name="layer",
    )(
        cached_len, hidden_in.T, freq, attn_gain.reshape(CHIPS, 128), ffn_gain.reshape(CHIPS, 128),
        k_cache[0], v_cache[0], wqkv, wo, wgate, wup, wdown,
    )
    out, nk, nv = pl.pallas_call(
        cache_kernel,
        out_shape=(
            jax.ShapeDtypeStruct((64, 2 * TOK), BF16),
            jax.ShapeDtypeStruct((SLOTS, HD), BF16),
            jax.ShapeDtypeStruct((SLOTS, HD), BF16),
        ),
        in_specs=[pl.BlockSpec(memory_space=pltpu.SMEM)] + [in_vmem] * 5,
        out_specs=(in_vmem, in_vmem, in_vmem),
        name="caches",
    )(cached_len, out, new_k, new_v, k_cache[0], v_cache[0])
    return (out.T, nk[None], nv[None])


def solution(mesh):
    return jax.shard_map(
        per_device,
        mesh=mesh,
        in_specs=(
            P("narrow", "wide"),
            P(),
            P("narrow", "wide", None),
            P("narrow", "wide", None),
            P(),
            P(),
            P("wide", "narrow"),
            P("wide", "narrow"),
            P("wide", "narrow"),
            P("wide", "narrow"),
            P("wide", "narrow"),
        ),
        out_specs=(P("narrow", "wide"), P("narrow", "wide", None), P("narrow", "wide", None)),
        check_vma=False,
    )
```

```python
import jax
import jax.numpy as jnp
import numpy as np
from jax import lax
from jax.experimental import pallas as pl
from jax.experimental.pallas import tpu as pltpu
from jax.sharding import PartitionSpec as P

HD = 128
WINDOW = 4096
NEG_FILL = -1e30
NZ, NY, NX = 8, 4, 4
CHIPS = NZ * NY
TOK = 128
SLOTS = 512
BF16 = jnp.bfloat16
F32 = jnp.float32
YORDER = (0, 1, 3, 2)
UP_FROM = 3
NEAR = (1, -1, 2, -2, 3, -3, 4)


def dot(a, b):
    return jnp.dot(a, b, preferred_element_type=F32)


def dot_nt(a, b):
    return lax.dot_general(a, b, (((1,), (1,)), ((), ())), preferred_element_type=F32)


def layer_kernel(
    len_ref, hid, freq_h, gain1_h, gain2_h, kc, vc, wqkv, wo, wg, wu, wd,
    out, new_k, new_v,
    freq, gain1, gain2, vl, l_sem, ht, cos, sin, xb, ab, hb, nb, gq, kvn, krt, ka, vt, sc, sn, ssq,
    wqf, wof, wgf, wuf, wdf, gb, pj, gu, db, total_f, ys, yr, zs, zr, fin, fin_r,
    p_s, p_r, ag_s, ag_r, w_l, w_s, w_r, kv_s, kv_r, q_s, q_r, rs_s, rs_r,
):
    wide = lax.axis_index("wide")
    x = lax.axis_index("narrow")
    k = wide % 2
    y = (wide // 2) % NY
    z = wide // (2 * NY)
    sg = 1 - 2 * k
    chip = z * NY + y

    def dev(zz, yy, kk, xx):
        return {"wide": (zz * NY + yy) * 2 + kk, "narrow": xx}

    def ypeer(d):
        return dev(z, (y + d) % NY, k, x)

    def zpeer(d):
        return dev((z + d + NZ) % NZ, y, k, x)

    partner = dev(z, y, 1 - k, x)
    za = (z + sg + NZ) % NZ
    zb = (z - sg + NZ) % NZ
    dev_a = dev(za, y, k, x)
    dev_b = dev(zb, y, k, x)
    xr = (x + 1) % NX
    xl = (x + NX - 1) % NX
    xo = (x + 2) % NX
    dev_xr = dev(z, y, k, xr)
    dev_xl = dev(z, y, k, xl)

    pending = []
    pending_w = {m: [] for m in range(5)}

    def drain(copies):
        for copy in copies:
            copy.wait_send()
        copies.clear()

    def send(src, dst, s_sem, r_sem, device, started=pending):
        copy = pltpu.make_async_remote_copy(
            src_ref=src, dst_ref=dst, send_sem=s_sem, recv_sem=r_sem,
            device_id=device, device_id_type=pl.DeviceIdType.MESH,
        )
        copy.start()
        started.append(copy)

    def arrive(dst, r_sem):
        pltpu.make_async_remote_copy(
            src_ref=dst, dst_ref=dst, send_sem=r_sem, recv_sem=r_sem,
            device_id=partner, device_id_type=pl.DeviceIdType.MESH,
        ).wait_recv()

    barrier = pltpu.get_barrier_semaphore()
    greet = [partner, ypeer(1), ypeer(2), ypeer(3), dev_xr, dev_xl] + [zpeer(d) for d in NEAR]
    for peer in greet:
        pl.semaphore_signal(barrier, inc=1, device_id=peer, device_id_type=pl.DeviceIdType.MESH)
    inward = [
        pltpu.make_async_copy(src, dst, l_sem.at[i])
        for i, (src, dst) in enumerate((
            (hid.at[:, pl.ds(0, TOK)], ht.at[0]), (hid.at[:, pl.ds(TOK, TOK)], ht.at[1]),
            (kc, ka.at[2 * y + k]), (vc, vl), (freq_h, freq), (gain1_h, gain1), (gain2_h, gain2),
        ))
    ]
    for copy in inward:
        copy.start()
    ssq[...] = jnp.zeros_like(ssq)
    pl.semaphore_wait(barrier, len(greet))

    own_w = (wqkv, wo, wg, wu, wd)
    full_w = (wqf, wof, wgf, wuf, wdf)
    locals_w = []

    def w_first(m):
        f, o = full_w[m], own_w[m]
        copy = pltpu.make_async_copy(o, f.at[x, k], w_l.at[m])
        copy.start()
        locals_w.append(copy)
        send(o, f.at[x, k], w_s.at[m, 0], w_r.at[m, 0], dev_xr, pending_w[m])
        send(o, f.at[x, k], w_s.at[m, 1], w_r.at[m, 1], dev_xl, pending_w[m])
        send(o, f.at[x, k], w_s.at[m, 4], w_r.at[m, 4], partner, pending_w[m])

    def w_second(m):
        f = full_w[m]
        half = f.shape[2] // 2
        lo, hi = pl.ds(0, half), pl.ds(half, half)
        arrive(f.at[xl, k], w_r.at[m, 0])
        send(f.at[xl, k, lo], f.at[xl, k, lo], w_s.at[m, 2], w_r.at[m, 2], dev_xr, pending_w[m])
        send(f.at[xl, k], f.at[xl, k], w_s.at[m, 5], w_r.at[m, 5], partner, pending_w[m])
        arrive(f.at[xr, k], w_r.at[m, 1])
        send(f.at[xr, k, hi], f.at[xr, k, hi], w_s.at[m, 3], w_r.at[m, 3], dev_xl, pending_w[m])
        send(f.at[xr, k], f.at[xr, k], w_s.at[m, 6], w_r.at[m, 6], partner, pending_w[m])

    def w_third(m):
        f = full_w[m]
        half = f.shape[2] // 2
        lo, hi = pl.ds(0, half), pl.ds(half, half)
        arrive(f.at[xo, k, lo], w_r.at[m, 2])
        arrive(f.at[xo, k, hi], w_r.at[m, 3])
        send(f.at[xo, k], f.at[xo, k], w_s.at[m, 7], w_r.at[m, 7], partner, pending_w[m])

    blocks = (x, xl, xr, xo)

    def w_ready(m, i):
        if i == 0:
            locals_w[m].wait()
        arrive(full_w[m].at[blocks[i], 1 - k], w_r.at[m, 4 + i])

    def rows_of(buf, i):
        return buf[pl.ds(pl.multiple_of(8 * blocks[i], 8), 8)].reshape(1024, TOK)

    def all_gather(g, buf, on_chunk, extra, pumps):
        send_sem, recv_sem = ag_s.at[g], ag_r.at[g]

        def a_sem(s, d):
            return 3 + (s - 1) * 4 + d

        def b_sem(s, d):
            return 19 + (s - 1) * 4 + d

        def row(zz, d):
            return ((zz + 2 * NZ) % NZ) * NY + (y + NY - d) % NY

        def push_a(s, d):
            ref = buf.at[row(z - sg * (s - 1), d)]
            send(ref, ref, send_sem.at[a_sem(s, d)], recv_sem.at[a_sem(s, d)], dev_a)

        def push_b(s, d):
            ref = buf.at[row(z + sg * (s - 1), d)]
            send(ref, ref, send_sem.at[b_sem(s, d)], recv_sem.at[b_sem(s, d)], dev_b)

        own = buf.at[chip]
        for d in (1, 3, 2):
            send(own, own, send_sem.at[d - 1], recv_sem.at[d - 1], ypeer(d))
        push_a(1, 0)
        push_b(1, 0)
        extra()
        on_chunk(chip)
        for d in YORDER[1:]:
            arrive(buf.at[row(z, d)], recv_sem.at[d - 1])
            push_a(1, d)
            push_b(1, d)
            on_chunk(row(z, d))
        for s in range(2, 6):
            for d in YORDER:
                c = row(z - sg * (s - 1), d)
                arrive(buf.at[c], recv_sem.at[a_sem(s - 1, d)])
                if s <= 4:
                    push_a(s, d)
                on_chunk(c)
                if s <= 4:
                    c = row(z + sg * (s - 1), d)
                    arrive(buf.at[c], recv_sem.at[b_sem(s - 1, d)])
                    if s <= 3:
                        push_b(s, d)
                    on_chunk(c)
                if (s, d) in pumps:
                    pumps[s, d]()

    def all_gather_direct(g, buf, on_chunk, extra, pumps, on_plane):
        send_sem, recv_sem = ag_s.at[g], ag_r.at[g]

        def row(dz, dy):
            return ((z + dz + NZ) % NZ) * NY + (y + dy + NY) % NY

        def y_sem(dz, d):
            return 8 + (dz % NZ) * 3 + d - 1

        def y_send(dz):
            ref = buf.at[row(dz, 0)]
            for d in (2, 1, 3):
                send(ref, ref, send_sem.at[y_sem(dz, d)], recv_sem.at[y_sem(dz, d)], ypeer(d))

        own = buf.at[chip]
        for dz in NEAR:
            send(own, own, send_sem.at[dz % NZ], recv_sem.at[dz % NZ], zpeer(dz))
        y_send(0)
        extra()
        on_chunk(chip)
        for dz in NEAR:
            arrive(buf.at[row(-dz, 0)], recv_sem.at[dz % NZ])
            y_send(-dz)
            on_chunk(row(-dz, 0))
        for i, dz in enumerate((0,) + NEAR):
            for d in (1, 3, 2):
                arrive(buf.at[row(-dz, -d)], recv_sem.at[y_sem(-dz, d)])
                on_chunk(row(-dz, -d))
            if i in pumps:
                pumps[i]()
            on_plane(i, (z - dz + NZ) % NZ)

    def add_square(buf):
        def run(c):
            v = buf[c].astype(F32)
            ssq[...] += jnp.sum((v * v).reshape(16, 8, TOK), axis=0)

        return run

    def normalise(buf, gain):
        mean_square = jnp.sum(ssq[...], axis=0, keepdims=True) * (1.0 / (CHIPS * 128))
        r = lax.rsqrt(mean_square + 1e-05)
        gains = jnp.transpose(gain[...].astype(F32))
        for c in range(CHIPS):
            nb[c] = (buf[c].astype(F32) * r * gains[:, c : c + 1]).astype(BF16)

    half_rows = pl.ds(pl.multiple_of(k * 64, 64), 64)
    other_rows = pl.ds(pl.multiple_of((1 - k) * 64, 64), 64)
    inward[0].wait()
    inward[1].wait()
    send(ht.at[1 - k], xb.at[chip, half_rows], p_s.at[0], p_r.at[0], partner)
    xb[chip, half_rows, :] = ht[k]
    w_first(0)
    w_first(1)
    arrive(xb.at[chip, other_rows], p_r.at[0])

    def send_caches():
        p = 2 * y + k
        for d in (1, 3, 2):
            send(ka.at[p], ka.at[p], kv_s.at[0, d - 1], kv_r.at[0, d - 1], ypeer(d))
            send(vt.at[p], vt.at[p], kv_s.at[1, d - 1], kv_r.at[1, d - 1], ypeer(d))
        send(ka.at[p], ka.at[p], kv_s.at[0, 3], kv_r.at[0, 3], partner)
        send(vt.at[p], vt.at[p], kv_s.at[1, 3], kv_r.at[1, 3], partner)

    def pass_caches():
        for d in (1, 3, 2):
            p = 2 * ((y + NY - d) % NY) + k
            for i, buf in enumerate((ka, vt)):
                arrive(buf.at[p], kv_r.at[i, d - 1])
                send(buf.at[p], buf.at[p], kv_s.at[i, 3 + d], kv_r.at[i, 3 + d], partner)

    def caches_ready():
        for d in range(NY):
            p = 2 * ((y + NY - d) % NY) + 1 - k
            for i, buf in enumerate((ka, vt)):
                arrive(buf.at[p], kv_r.at[i, 3 + d])

    def before_first():
        for copy in inward[2:]:
            copy.wait()
        vt[2 * y + k] = jnp.transpose(vl[...].astype(F32)).astype(BF16)
        send_caches()
        for h in range(2):
            t = lax.broadcasted_iota(jnp.int32, (1, TOK), 1) + (TOK * h + len_ref[x])
            angle = freq[:, 0:1] * t.astype(F32)
            cos[h] = jnp.cos(angle)
            sin[h] = jnp.sin(angle)

    def pump_first():
        w_second(0)
        w_first(2)

    def pump_second():
        w_second(1)
        w_first(3)

    def pump_third():
        w_third(0)

    all_gather(
        0, xb, add_square(xb), before_first,
        {(2, 2): pump_first, (3, 2): pump_second, (5, 1): pump_third},
    )
    normalise(xb, gain1)
    rows_q = wqf.shape[2] * 2
    acc = jnp.zeros((rows_q, TOK), F32)
    for i in range(NX):
        w_ready(0, i)
        acc += dot(wqf[blocks[i]].reshape(rows_q, 1024), rows_of(nb, i))
    gq[y] = acc.astype(BF16)

    for d in (1, 3, 2):
        send(gq.at[y], gq.at[y], q_s.at[d - 1], q_r.at[d - 1], ypeer(d))
    pass_caches()
    for d in (1, 3, 2):
        arrive(gq.at[(y + NY - d) % NY], q_r.at[d - 1])
    grouped = gq[...].reshape(NY * rows_q, TOK)
    kvn[k] = grouped[4 * HD :]
    send(kvn.at[k], kvn.at[k], q_s.at[3], q_r.at[3], partner)

    def rotate(v, cosine, sine):
        v = v.astype(F32)
        a, b = v[:64], v[64:]
        return jnp.concatenate([a * cosine - b * sine, b * cosine + a * sine], axis=0)

    sn[...] = jnp.zeros_like(sn)
    for head in range(NY):

        @pl.when(y == head)
        def _():
            sn[0] = rotate(grouped[head * HD : (head + 1) * HD], cos[k], sin[k])

    qt = sn[0].astype(BF16)
    length = len_ref[x]
    t_row = lax.broadcasted_iota(jnp.int32, (1, TOK), 1) + TOK * k
    caches_ready()

    def cache_scores(b, peak):
        s = dot(ka[b], qt) * HD ** (-0.5)
        slot = lax.broadcasted_iota(jnp.int32, (SLOTS, 1), 0) + b * SLOTS
        allowed = (slot < length) & (slot > length + t_row - WINDOW)
        s = jnp.where(allowed, s, NEG_FILL)
        sc[b] = s
        return jnp.maximum(peak, jnp.max(s, axis=0, keepdims=True))

    peak = lax.fori_loop(0, WINDOW // SLOTS, cache_scores, jnp.full((1, TOK), NEG_FILL, F32))
    arrive(kvn.at[1 - k], q_r.at[3])
    for h in range(2):
        kt = rotate(kvn[h, :HD], cos[h], sin[h])
        krt[h] = kt.astype(BF16)
        s = dot(jnp.transpose(kt).astype(BF16), qt) * HD ** (-0.5)
        t2 = lax.broadcasted_iota(jnp.int32, (TOK, 1), 0) + TOK * h
        s = jnp.where(t2 <= t_row, s, NEG_FILL)
        sn[h] = s
        peak = jnp.maximum(peak, jnp.max(s, axis=0, keepdims=True))

    def cache_mix(b, carry):
        total, mixed = carry
        e = jnp.exp(sc[b] - peak)
        return (total + jnp.sum(e, axis=0, keepdims=True), mixed + dot(vt[b], e.astype(BF16)))

    total, mixed = lax.fori_loop(
        0, WINDOW // SLOTS, cache_mix, (jnp.zeros((1, TOK), F32), jnp.zeros((HD, TOK), F32))
    )
    for h in range(2):
        e = jnp.exp(sn[h] - peak)
        total = total + jnp.sum(e, axis=0, keepdims=True)
        mixed = mixed + dot(kvn[h, HD:], e.astype(BF16))
    ab[chip] = (mixed / total).astype(BF16)

    count_first = len(pending)
    rows_o = wof.shape[2] * 2
    rows_f = wgf.shape[2] * 2

    def plane_of(f, rows, zz):
        cols = pl.ds(pl.multiple_of((zz % 2) * 512, 512), 512)
        return f[zz // 2, :, :, cols].reshape(rows, 512)

    def plane_rows(buf, zz):
        return buf[pl.ds(pl.multiple_of(NY * zz, NY), NY)].reshape(NY * 128, TOK)

    def project(i, zz):
        if i == 0:
            for j in range(NX):
                w_ready(1, j)
        part = dot(plane_of(wof, rows_o, zz), plane_rows(ab, zz))
        pj[...] = part if i == 0 else pj[...] + part

    def up_then_down():
        w_second(3)
        w_first(4)

    def before_second():
        w_second(2)
        w_third(1)
        drain(pending[:count_first])
        del pending[:count_first]
        gains = jnp.transpose(gain2[...].astype(F32))
        for c in range(CHIPS):
            gb[c] = jnp.broadcast_to(gains[:, c : c + 1], (128, TOK))
        for h in range(2):
            new_k[h] = krt[h]
            new_v[h] = kvn[h, HD:]

    all_gather_direct(
        1, ab, lambda c: None, before_second,
        {4: up_then_down, 7: lambda: w_third(2)}, project,
    )
    hb[chip] = (xb[chip].astype(F32) + pj[...]).astype(BF16)
    ssq[...] = jnp.zeros_like(ssq)

    count_second = len(pending)

    def before_third():
        drain(pending[:count_second])
        del pending[:count_second]
        drain(pending_w[0])
        drain(pending_w[1])

    def square_and_gain(c):
        v = hb[c].astype(F32)
        ssq[...] += jnp.sum((v * v).reshape(16, 8, TOK), axis=0)
        nb[c] = (v * gb[c]).astype(BF16)

    def hidden_part(m, f, i, zz):
        part = dot(plane_of(f, rows_f, zz), plane_rows(nb, zz))
        gu[m] = part if i == 0 else gu[m] + part

    planes = []

    def hidden_plane(i, zz):
        planes.append(zz)
        if i == 0:
            for j in range(NX):
                w_ready(2, j)
        hidden_part(0, wgf, i, zz)
        if i == UP_FROM:
            for j in range(NX):
                w_ready(3, j)
            for n in range(i):
                hidden_part(1, wuf, n, planes[n])
        if i >= UP_FROM:
            hidden_part(1, wuf, i, zz)

    all_gather_direct(
        2, hb, square_and_gain, before_third,
        {0: lambda: w_third(3), 6: lambda: w_second(4)}, hidden_plane,
    )
    r = lax.rsqrt(jnp.sum(ssq[...], axis=0, keepdims=True) * (1.0 / (CHIPS * 128)) + 1e-05)
    gate = gu[0] * r
    act = (gate / (1.0 + jnp.exp(-gate))) * (gu[1] * r)
    act_t = jnp.transpose(act).astype(BF16)

    count_third = len(pending)

    for i in range(NZ):
        block = blocks[i // 2]
        if i == 4:
            w_third(4)
        if i % 2 == 0:
            w_ready(4, i // 2)
        cols = pl.ds((i % 2) * 512, 512)
        db[i] = dot(act_t, wdf[block, :, :, cols].reshape(rows_f, 512))
        for d in (2, 1, 3):
            col = pl.ds(pl.multiple_of(((y + d) % NY) * 128, 128), 128)
            ys[i, d - 1] = db[i, :, col].astype(BF16)
            n = 3 * i + d - 1
            send(ys.at[i, d - 1], yr.at[i, d - 1], rs_s.at[n], rs_r.at[n], ypeer(d))
    own_col = pl.ds(pl.multiple_of(y * 128, 128), 128)
    drain(pending[:count_third])
    del pending[:count_third]
    drain(pending_w[2])
    drain(pending_w[3])
    for i in range(NZ):
        zz = 2 * blocks[i // 2] + i % 2
        disp = (zz - z + NZ) % NZ
        v = db[i, :, own_col]
        for d in (1, 3, 2):
            arrive(yr.at[i, d - 1], rs_r.at[3 * i + d - 1])
            v = v + yr[i, d - 1].astype(F32)
        zs[disp] = v.astype(BF16)

        @pl.when(disp == 0)
        def _():
            total_f[...] = v

        @pl.when(disp != 0)
        def _():
            pltpu.make_async_remote_copy(
                src_ref=zs.at[disp], dst_ref=zr.at[disp],
                send_sem=rs_s.at[23 + disp], recv_sem=rs_r.at[23 + disp],
                device_id=dev(zz, y, k, x), device_id_type=pl.DeviceIdType.MESH,
            ).start()

    whole = total_f[...]
    for dz in NEAR:
        arrive(zr.at[dz % NZ], rs_r.at[23 + dz % NZ])
        whole = whole + zr[dz % NZ].astype(F32)
    fin[...] = (hb[chip].astype(F32) + jnp.transpose(whole)).astype(BF16)
    send(fin.at[other_rows], fin_r, rs_s.at[31], rs_r.at[31], partner)
    out[:, pl.ds(pl.multiple_of(k * TOK, TOK), TOK)] = fin[half_rows, :]
    arrive(fin_r, rs_r.at[31])
    out[:, pl.ds(pl.multiple_of((1 - k) * TOK, TOK), TOK)] = fin_r[...]
    drain(pending)
    drain(pending_w[4])
    for i in range(1, NZ):
        pltpu.make_async_remote_copy(
            src_ref=zs.at[i], dst_ref=zr.at[i], send_sem=rs_s.at[23 + i], recv_sem=rs_r.at[23 + i],
            device_id=partner, device_id_type=pl.DeviceIdType.MESH,
        ).wait_send()


def cache_kernel(len_ref, hid, new_k, new_v, kc, vc, out, nk, nv):
    length = len_ref[lax.axis_index("narrow")]
    slot = lax.broadcasted_iota(jnp.int32, (SLOTS, TOK), 0) + lax.axis_index("wide") % 8 * SLOTS
    offset = slot - length
    offset = jnp.where(offset < 0, offset + WINDOW, offset)
    lane = lax.broadcasted_iota(jnp.int32, (SLOTS, TOK), 1)
    first = jnp.where(offset == lane, 1.0, 0.0).astype(BF16)
    second = jnp.where(offset == lane + TOK, 1.0, 0.0).astype(BF16)
    fresh = offset < 2 * TOK
    keys = dot_nt(first, new_k[0]) + dot_nt(second, new_k[1])
    vals = dot_nt(first, new_v[0]) + dot_nt(second, new_v[1])
    nk[...] = jnp.where(fresh, keys, kc[...].astype(F32)).astype(BF16)
    nv[...] = jnp.where(fresh, vals, vc[...].astype(F32)).astype(BF16)
    out[...] = hid[...]


def per_device(
    hidden_in, cached_len, k_cache, v_cache, attn_gain, ffn_gain, wqkv, wo, wgate, wup, wdown
):
    exponent = np.arange(HD // 2, dtype=np.float32) * np.float32(2.0 / HD)
    frequency = np.power(np.float32(10000.0), -exponent).astype(np.float32)
    freq = jnp.asarray(np.outer(frequency, np.arange(1, TOK + 1, dtype=np.float32)))

    def vm(*shape, dtype=BF16):
        return pltpu.VMEM(shape, dtype)

    def sems(*shape):
        return pltpu.SemaphoreType.DMA(shape)

    def full(w):
        return vm(NX, 2, w.shape[0], w.shape[1])

    in_vmem = pl.BlockSpec(memory_space=pltpu.VMEM)
    in_hbm = pl.BlockSpec(memory_space=pl.ANY)
    out, new_k, new_v = pl.pallas_call(
        layer_kernel,
        out_shape=(
            jax.ShapeDtypeStruct((64, 2 * TOK), BF16),
            jax.ShapeDtypeStruct((2, HD, TOK), BF16),
            jax.ShapeDtypeStruct((2, HD, TOK), BF16),
        ),
        in_specs=[pl.BlockSpec(memory_space=pltpu.SMEM)] + [in_hbm] * 11,
        out_specs=(in_vmem, in_vmem, in_vmem),
        scratch_shapes=[
            vm(HD // 2, TOK, dtype=F32), vm(CHIPS, 128), vm(CHIPS, 128), vm(SLOTS, HD), sems(7),
            vm(2, 64, TOK), vm(2, 64, TOK, dtype=F32), vm(2, 64, TOK, dtype=F32),
            vm(CHIPS, 128, TOK), vm(CHIPS, 128, TOK), vm(CHIPS, 128, TOK), vm(CHIPS, 128, TOK),
            vm(NY, 2 * wqkv.shape[0], TOK), vm(2, 2 * HD, TOK), vm(2, HD, TOK),
            vm(8, SLOTS, HD), vm(8, HD, SLOTS),
            vm(8, SLOTS, TOK, dtype=F32), vm(2, TOK, TOK, dtype=F32), vm(8, TOK, dtype=F32),
            full(wqkv), full(wo), full(wgate), full(wup), full(wdown),
            vm(CHIPS, 128, TOK, dtype=F32), vm(128, TOK, dtype=F32),
            vm(2, 2 * wgate.shape[0], TOK, dtype=F32),
            vm(NZ, TOK, 512, dtype=F32), vm(TOK, 128, dtype=F32),
            vm(NZ, 3, TOK, 128), vm(NZ, 3, TOK, 128), vm(NZ, TOK, 128), vm(NZ, TOK, 128),
            vm(128, TOK), vm(64, TOK),
            sems(1), sems(1), sems(3, 32), sems(3, 32), sems(5), sems(5, 8), sems(5, 8),
            sems(2, 7), sems(2, 7), sems(4), sems(4), sems(32), sems(32),
        ],
        compiler_params=pltpu.CompilerParams(
            collective_id=0, has_side_effects=True, vmem_limit_bytes=60 * 1024 * 1024
        ),
        name="layer",
    )(
        cached_len, hidden_in.T, freq, attn_gain.reshape(CHIPS, 128), ffn_gain.reshape(CHIPS, 128),
        k_cache[0], v_cache[0], wqkv, wo, wgate, wup, wdown,
    )
    out, nk, nv = pl.pallas_call(
        cache_kernel,
        out_shape=(
            jax.ShapeDtypeStruct((64, 2 * TOK), BF16),
            jax.ShapeDtypeStruct((SLOTS, HD), BF16),
            jax.ShapeDtypeStruct((SLOTS, HD), BF16),
        ),
        in_specs=[pl.BlockSpec(memory_space=pltpu.SMEM)] + [in_vmem] * 5,
        out_specs=(in_vmem, in_vmem, in_vmem),
        name="caches",
    )(cached_len, out, new_k, new_v, k_cache[0], v_cache[0])
    return (out.T, nk[None], nv[None])


def solution(mesh):
    return jax.shard_map(
        per_device,
        mesh=mesh,
        in_specs=(
            P("narrow", "wide"),
            P(),
            P("narrow", "wide", None),
            P("narrow", "wide", None),
            P(),
            P(),
            P("wide", "narrow"),
            P("wide", "narrow"),
            P("wide", "narrow"),
            P("wide", "narrow"),
            P("wide", "narrow"),
        ),
        out_specs=(P("narrow", "wide"), P("narrow", "wide", None), P("narrow", "wide", None)),
        check_vma=False,
    )
```
